256 devices in a mesh: fsdp: 64 (over y, z, core), tp: 4 (over x).
Axes of the slice: x: 4, y: 4, z: 8, core: 2. Of those that a mesh axis runs over, the one named last changes fastest.
Arguments:
- grads: float32 [4, 512, 256, 256], P('tp', None, 'fsdp'), may hold values from -200 to 200
- weights: float32 [512, 256, 256], P('tp', 'fsdp'), may hold values from -0.3 to 0.3
- moments: float32 [512, 256, 256], P('tp', 'fsdp'), may hold values from 0.05 to 2
- left_stat: float32 [4, 64, 6, 256, 256], P('tp', 'fsdp'), may hold values from -20 to 200
- right_stat: float32 [4, 64, 6, 256, 256], P('tp', 'fsdp'), may hold values from -20 to 200
- left_root: bfloat16 [4, 64, 6, 256, 256], P('tp', 'fsdp'), may hold values from -1 to 2
- right_root: bfloat16 [4, 64, 6, 256, 256], P('tp', 'fsdp'), may hold values from -1 to 2
- owner: int32 [512], P('tp'), may hold values from 0 to 63, as said below
- extent: int32 [512, 2], P('tp'), may hold values from 1 to 2
Outputs:
- new_weights: float32 [512, 256, 256], P('tp', 'fsdp')
- new_moments: float32 [512, 256, 256], P('tp', 'fsdp')
- new_left: float32 [4, 64, 6, 256, 256], P('tp', 'fsdp')
- new_right: float32 [4, 64, 6, 256, 256], P('tp', 'fsdp')
The draws below stay inside these ranges and needn't reach their ends.
Inputs may be any that keep to these rules, and one draw needn't show every extreme that they name: `owner`: within each group of 128 consecutive blocks, no device owns more than 6 blocks, and some device owns exactly 6.
All inputs are finite; a program needn't handle non-finite values.
Results may differ from the reference program's by a relative error of at most 0.0003.
Values sent between devices are 32-bit elements; how exact they have to be, the bound alone decides.
A program may use at most 64 MiB of HBM per device.

```python
import math
import jax
import jax.numpy as jnp
from jax import lax

BLOCK = 256
OWN_DEV = 2
OWNERS = 64
COL_BLOCKS = 128
NBLK = 512
LOAD_MAX = 6
N_TP = 4


def symmetric_draw(key, shape, diag_lo, diag_hi, spread):
    noise_key, diag_key = jax.random.split(key)
    noise = jnp.clip(jax.random.normal(noise_key, shape, jnp.float32), -6.0, 6.0)
    paired = (noise + jnp.swapaxes(noise, -1, -2)) * (spread / math.sqrt(2.0 * BLOCK))
    diagonal = jnp.exp(jax.random.uniform(diag_key, shape[:-1], jnp.float32, math.log(diag_lo), math.log(diag_hi)))
    identity = (jnp.arange(BLOCK)[:, None] == jnp.arange(BLOCK)[None, :]).astype(jnp.float32)
    return paired * (1.0 - identity) + identity * diagonal[..., :, None]


def draw_grads(key, part):
    shape = (N_TP, NBLK, BLOCK, BLOCK)
    noise_key, row_key, col_key = jax.random.split(key, 3)
    noise = jnp.clip(jax.random.normal(noise_key, shape, jnp.float32), -6.0, 6.0)
    trend = jnp.exp(math.log(3.0) * jnp.arange(BLOCK, dtype=jnp.float32) / BLOCK)
    row_rand = jnp.exp(jax.random.uniform(row_key, (1, NBLK, BLOCK, 1), jnp.float32, 0.0, math.log(3.0)))
    col_rand = jnp.exp(jax.random.uniform(col_key, (1, NBLK, 1, BLOCK), jnp.float32, 0.0, math.log(10.0)))
    return noise * trend[None, None, :, None] * row_rand * col_rand * 0.25


def draw_left_stat(key, part):
    return symmetric_draw(jax.random.fold_in(key, 11), (N_TP, OWNERS, LOAD_MAX, BLOCK, BLOCK), 20.0, 200.0, 10.0)


def draw_right_stat(key, part):
    return symmetric_draw(jax.random.fold_in(key, 12), (N_TP, OWNERS, LOAD_MAX, BLOCK, BLOCK), 20.0, 200.0, 10.0)


def draw_left_root(key, part):
    return symmetric_draw(jax.random.fold_in(key, 13), (N_TP, OWNERS, LOAD_MAX, BLOCK, BLOCK), 0.5, 2.0, 0.5).astype(jnp.bfloat16)


def draw_right_root(key, part):
    return symmetric_draw(jax.random.fold_in(key, 14), (N_TP, OWNERS, LOAD_MAX, BLOCK, BLOCK), 0.5, 2.0, 0.5).astype(jnp.bfloat16)


def owner_column(column_key):
    order_key, shuffle_key = jax.random.split(column_key)
    owner_order = jax.random.permutation(order_key, OWNERS).astype(jnp.int32)
    position = jnp.arange(COL_BLOCKS, dtype=jnp.int32)
    bound_one = 3 * OWN_DEV * (OWNERS // 8)
    bound_two = bound_one + OWN_DEV * (3 * OWNERS // 8)
    ranked = jnp.where(position < bound_one, position // (3 * OWN_DEV), jnp.where(position < bound_two, OWNERS // 8 + (position - bound_one) // OWN_DEV, OWNERS // 2 + (position - bound_two) // (OWN_DEV // 2)))
    listed = owner_order[ranked]
    return listed[jax.random.permutation(shuffle_key, COL_BLOCKS)]


def draw_owner(key, part):
    column_keys = jax.random.split(jax.random.fold_in(key, 21), NBLK // COL_BLOCKS)
    return jax.vmap(owner_column)(column_keys).reshape(NBLK).astype(jnp.int32)


def plant(result, own_key, smallest, largest):
    place = [jax.random.randint(jax.random.fold_in(own_key, axis), (), 0, length) for axis, length in enumerate(result.shape)]
    main_axis = result.shape.index(max(result.shape))
    next_to = place[:main_axis] + [(place[main_axis] + 1) % result.shape[main_axis]] + place[main_axis + 1:]
    return result.at[tuple(place)].set(smallest).at[tuple(next_to)].set(largest)


def shard_levels(key, shape, pieces, least, high):
    def one(dim, parts):
        heights = jax.random.uniform(jax.random.fold_in(jax.random.fold_in(key, 6), dim), (parts,), jnp.float32, least / len(pieces), high / len(pieces))
        return jnp.repeat(jnp.exp(heights), shape[dim] // parts).reshape((-1,) + (1,) * (len(shape) - dim - 1))

    loudness = one(*pieces[0])
    for cut in pieces[1:]:
        loudness = loudness * one(*cut)
    return loudness


def normal_values(own_key, shape, scale, reach, pieces=(), kind=jnp.bfloat16):
    level = shard_levels(own_key, shape, pieces, -0.22, 0.18) if pieces else 1.0
    result = jax.random.normal(own_key, shape, jnp.float32) * scale * level
    return jnp.minimum(jnp.maximum(result, -reach), reach).astype(kind)


def setup_inputs(seed: int = 0) -> dict:
    key_list = jax.random.split(jax.random.key(seed), 10)
    grads = draw_grads(jax.random.fold_in(key_list[9], 71), 0)
    weights = normal_values(key_list[1], (NBLK, BLOCK, BLOCK), 0.05, 0.3, ((0, 4), (1, 64)), jnp.float32)
    moments = jnp.clip(jnp.exp(math.log(2.0) - 3.6888794 * jax.random.uniform(key_list[2], (NBLK, BLOCK, BLOCK), jnp.float32) ** shard_levels(key_list[2], (NBLK, BLOCK, BLOCK), ((0, 4), (1, 64)), -0.2, 0.2)), 0.05, 2.0)
    left_stat = draw_left_stat(jax.random.fold_in(key_list[9], 71), 0)
    right_stat = draw_right_stat(jax.random.fold_in(key_list[9], 71), 0)
    left_root = draw_left_root(jax.random.fold_in(key_list[9], 71), 0)
    right_root = draw_right_root(jax.random.fold_in(key_list[9], 71), 0)
    owner = draw_owner(jax.random.fold_in(key_list[9], 71), 0)
    extent = plant(jax.random.randint(key_list[8], (NBLK, 2), 1, 3), jax.random.fold_in(key_list[8], 1), 1, 2).astype(jnp.int32)
    return {"grads": grads, "weights": weights, "moments": moments, "left_stat": left_stat, "right_stat": right_stat, "left_root": left_root, "right_root": right_root, "owner": owner, "extent": extent}


PRECISE = lax.Precision.HIGHEST
ADAM_BETA = 0.95
STAT_BETA = 0.99
LEARN_RATE = 0.05
ADAM_EPS = 1e-08
NORM_EPS = 1e-06

def extent_mask(extents, row_ids, col_ids, half_size):
    row_live = row_ids[None, :] < extents[:, 0:1] * half_size
    col_live = col_ids[None, :] < extents[:, 1:2] * half_size
    return (row_live[:, :, None] & col_live[:, None, :]).astype(jnp.float32)

def slot_tables(owner_col, owners, load_max):
    column = owner_col.shape[0]
    onehot = (owner_col[:, None] == jnp.arange(owners, dtype=jnp.int32)[None, :]).astype(jnp.int32)
    slot_rank = lax.optimization_barrier(jnp.sum((jnp.cumsum(onehot, axis=0) - onehot) * onehot, axis=1))
    flat_slot = owner_col * load_max + slot_rank
    slot_hits = flat_slot[:, None] == jnp.arange(owners * load_max, dtype=jnp.int32)[None, :]
    valid_slot = jnp.any(slot_hits, axis=0)
    block_index = lax.optimization_barrier(jnp.sum(jnp.where(slot_hits, jnp.arange(column, dtype=jnp.int32)[:, None], 0), axis=0)).astype(jnp.int32)
    return (flat_slot, valid_slot, block_index)

def refresh(slot_grad, left_old, right_old, left_inv, right_inv, slot_mask):
    left_prod = jnp.einsum('sij,skj->sik', slot_grad, slot_grad, precision=PRECISE)
    right_prod = jnp.einsum('sji,sjk->sik', slot_grad, slot_grad, precision=PRECISE)
    left_new = STAT_BETA * left_old + (1.0 - STAT_BETA) * left_prod
    right_new = STAT_BETA * right_old + (1.0 - STAT_BETA) * right_prod
    inner = jnp.einsum('sij,sjk->sik', left_inv.astype(jnp.float32), slot_grad, precision=PRECISE)
    precond = jnp.einsum('sij,sjk->sik', inner, right_inv.astype(jnp.float32), precision=PRECISE) * slot_mask
    return (left_new, right_new, precond)

def per_column(inputs):
    grad_col, left_old, right_old, left_inv, right_inv, owner_col, extent_col = inputs
    flat_slot, valid_slot, block_index = slot_tables(owner_col, OWNERS, LOAD_MAX)
    slot_grad = jnp.take(grad_col, block_index, axis=0) * valid_slot[:, None, None].astype(grad_col.dtype)
    full_ids = jnp.arange(BLOCK, dtype=jnp.int32)
    slot_mask = extent_mask(jnp.take(extent_col, block_index, axis=0), full_ids, full_ids, BLOCK // 2).astype(grad_col.dtype)
    flat_shape = (OWNERS * LOAD_MAX, BLOCK, BLOCK)
    left_new, right_new, precond = refresh(slot_grad, left_old.reshape(flat_shape), right_old.reshape(flat_shape), left_inv.reshape(flat_shape), right_inv.reshape(flat_shape), slot_mask)
    prec_blocks = jnp.take(precond, flat_slot, axis=0)
    return (left_new.reshape(left_old.shape), right_new.reshape(right_old.shape), prec_blocks)

def reference(grads, weights, moments, left_stat, right_stat, left_root, right_root, owner, extent):
    full_ids = jnp.arange(BLOCK, dtype=jnp.int32)
    block_mask = extent_mask(extent, full_ids, full_ids, BLOCK // 2).astype(grads.dtype)
    summed = lax.optimization_barrier(jnp.sum(grads, axis=0)) * block_mask
    new_moments = ADAM_BETA * moments + (1.0 - ADAM_BETA) * summed * summed
    adam_dir = summed / (jnp.sqrt(new_moments) + ADAM_EPS)
    adam_sq = lax.optimization_barrier(jnp.sum(adam_dir * adam_dir, axis=(1, 2)))
    groups = summed.shape[0] // COL_BLOCKS
    packed = (summed.reshape(groups, COL_BLOCKS, BLOCK, BLOCK), left_stat, right_stat, left_root, right_root, owner.reshape(groups, COL_BLOCKS), extent.reshape(groups, COL_BLOCKS, 2))
    new_left, new_right, prec_blocks = lax.map(per_column, packed)
    prec_blocks = prec_blocks.reshape(summed.shape)
    prec_sq = lax.optimization_barrier(jnp.sum(prec_blocks * prec_blocks, axis=(1, 2)))
    graft = jnp.sqrt(adam_sq / (prec_sq + NORM_EPS))
    new_weights = weights - LEARN_RATE * prec_blocks * graft[:, None, None]
    return (new_weights, new_moments, new_left, new_right)
```

```python
import jax
import jax.numpy as jnp
from jax import lax
from jax.sharding import PartitionSpec as P

PRECISE = lax.Precision.HIGHEST
ADAM_BETA = 0.95
STAT_BETA = 0.99
LEARN_RATE = 0.05
ADAM_EPS = 1e-08
NORM_EPS = 1e-06


def extent_mask(extents, row_ids, col_ids, half_size):
    row_live = row_ids[None, :] < extents[:, 0:1] * half_size
    col_live = col_ids[None, :] < extents[:, 1:2] * half_size
    return (row_live[:, :, None] & col_live[:, None, :]).astype(jnp.float32)


def slot_tables(owner_col, owners, load_max):
    column = owner_col.shape[0]
    onehot = (owner_col[:, None] == jnp.arange(owners, dtype=jnp.int32)[None, :]).astype(jnp.int32)
    slot_rank = jnp.sum((jnp.cumsum(onehot, axis=0) - onehot) * onehot, axis=1)
    flat_slot = owner_col * load_max + slot_rank
    slot_hits = flat_slot[:, None] == jnp.arange(owners * load_max, dtype=jnp.int32)[None, :]
    valid_slot = jnp.any(slot_hits, axis=0)
    block_index = jnp.sum(
        jnp.where(slot_hits, jnp.arange(column, dtype=jnp.int32)[:, None], 0), axis=0
    )
    return (flat_slot, valid_slot, block_index)


def refresh(slot_grad, left_old, right_old, left_inv, right_inv, slot_mask):
    left_prod = jnp.einsum("sij,skj->sik", slot_grad, slot_grad, precision=PRECISE)
    right_prod = jnp.einsum("sji,sjk->sik", slot_grad, slot_grad, precision=PRECISE)
    left_new = STAT_BETA * left_old + (1.0 - STAT_BETA) * left_prod
    right_new = STAT_BETA * right_old + (1.0 - STAT_BETA) * right_prod
    inner = jnp.einsum("sij,sjk->sik", left_inv.astype(jnp.float32), slot_grad, precision=PRECISE)
    precond = (
        jnp.einsum("sij,sjk->sik", inner, right_inv.astype(jnp.float32), precision=PRECISE)
        * slot_mask
    )
    return (left_new, right_new, precond)


def on_device(grads, weights, moments, left_stat, right_stat, left_root, right_root, owner, extent):
    owners = lax.axis_size("fsdp")
    my_index = lax.axis_index("fsdp")
    count_blocks, shard_rows, block_size = weights.shape
    load_max = left_stat.shape[2]
    half_size = block_size // 2
    tp_size = lax.axis_size("tp")
    parts = lax.all_to_all(
        grads[0].reshape(tp_size, count_blocks, shard_rows, block_size), "tp", split_axis=0, concat_axis=0, tiled=True
    )
    summed = jnp.sum(parts, axis=0)
    row_ids = my_index * shard_rows + jnp.arange(shard_rows, dtype=jnp.int32)
    col_ids = jnp.arange(block_size, dtype=jnp.int32)
    summed = summed * extent_mask(extent, row_ids, col_ids, half_size)
    new_moment = ADAM_BETA * moments + (1.0 - ADAM_BETA) * summed * summed
    adam_dir = summed / (jnp.sqrt(new_moment) + ADAM_EPS)
    adam_part = jnp.sum(adam_dir * adam_dir, axis=(1, 2))
    flat_slot, valid_slot, block_index = slot_tables(owner, owners, load_max)
    live = valid_slot.astype(jnp.float32)
    adam_out = (jnp.take(adam_part, block_index) * live).reshape(owners, load_max)
    adam_in = lax.all_to_all(adam_out, "fsdp", split_axis=0, concat_axis=0, tiled=True)
    adam_total = jnp.sum(adam_in, axis=0)
    outgoing = jnp.take(summed, block_index, axis=0) * valid_slot[:, None, None].astype(jnp.float32)
    outgoing = outgoing.reshape(owners, load_max, shard_rows, block_size)
    incoming = lax.all_to_all(outgoing, "fsdp", split_axis=0, concat_axis=2, tiled=True)[0]
    mine_index = lax.dynamic_slice_in_dim(block_index, my_index * load_max, load_max)
    mine_extent = jnp.take(extent, mine_index, axis=0)
    out_mask = extent_mask(mine_extent, col_ids, col_ids, half_size)
    left_new, right_new, precond = refresh(
        incoming, left_stat[0, 0], right_stat[0, 0], left_root[0, 0], right_root[0, 0], out_mask
    )
    prec_owner = jnp.sum(precond * precond, axis=(1, 2))
    graft = LEARN_RATE * jnp.sqrt(adam_total / (prec_owner + NORM_EPS))
    back_prec = lax.all_to_all(
        (precond * graft[:, None, None])[None], "fsdp", split_axis=2, concat_axis=0, tiled=True
    )
    home_prec = jnp.take(
        back_prec.reshape(owners * load_max, shard_rows, block_size), flat_slot, axis=0
    )
    new_weight = weights - home_prec
    return (new_weight, new_moment, left_new[None, None], right_new[None, None])


def solution(mesh):
    in_specs = (
        P("tp", None, "fsdp", None),
        P("tp", "fsdp", None),
        P("tp", "fsdp", None),
        P("tp", "fsdp", None, None, None),
        P("tp", "fsdp", None, None, None),
        P("tp", "fsdp", None, None, None),
        P("tp", "fsdp", None, None, None),
        P("tp"),
        P("tp", None),
    )
    out_specs = (
        P("tp", "fsdp", None),
        P("tp", "fsdp", None),
        P("tp", "fsdp", None, None, None),
        P("tp", "fsdp", None, None, None),
    )
    return jax.shard_map(
        on_device, mesh=mesh, in_specs=in_specs, out_specs=out_specs, check_vma=False
    )
```

```python
import functools

import jax
import jax.numpy as jnp
from jax import lax
from jax.experimental import pallas as pl
from jax.experimental.pallas import tpu as pltpu
from jax.sharding import PartitionSpec as P

ADAM_BETA = 0.95
STAT_BETA = 0.99
LEARN_RATE = 0.05
ADAM_EPS = 1e-08
NORM_EPS = 1e-06

NX, NY, NZ, NC = 4, 4, 8, 2
NYC = NY * NC
COLUMN = 128
SLOTS = 6
HALF = 128
MESH = pl.DeviceIdType.MESH
Z_ORDER = (4, 3, 5, 2, 6, 1, 7, 0)
F32 = jnp.float32
BF16 = jnp.bfloat16


def split(value):
    high = value.astype(BF16)
    low = (value - high.astype(F32)).astype(BF16)
    return high, low


def dot(a, b, dims=((1,), (0,))):
    return lax.dot_general(a, b, (dims, ((), ())), preferred_element_type=F32)


def step_kernel(
    cap,
    zpack, ypack, bpack, home, own_info,
    mask, own_hot, grads, moments, weights, left, right, left_root, right_root,
    new_w, new_m, new_left, new_right,
    *scratch,
):
    scratch = list(scratch)
    zr = [[scratch.pop(0) for _ in range(NZ)] for _ in range(2)]
    ybr = [scratch.pop(0) for _ in range(NZ)]
    summed = [scratch.pop(0) for _ in range(2)]
    (own_part, parts, mom, mom_out, arow, zsb, ysb, yr, gfull, lroot, rroot, lstat, rstat,
     ybs, zbs, zbr, wbuf,
     rs_send, rs_recv, z_send, z_recv, y_send, y_recv, yb_send, yb_recv, zb_send, zb_recv,
     loc_sem, in_sem, out_sem) = scratch

    me = lax.axis_index("fsdp")
    my_x = lax.axis_index("tp")
    my_c = lax.rem(me, NC)
    my_z = lax.rem(lax.div(me, NC), NZ)
    my_y = lax.div(me, NC * NZ)
    my_yc = my_y * NC + my_c

    def index_of(y, z, c):
        return (y * NZ + z) * NC + c

    def z_peer(d):
        return {"fsdp": index_of(my_y, lax.rem(my_z + d, NZ), my_c)}

    def yc_at(e):
        return lax.rem(my_y + e // NC, NY), lax.rem(my_c + e % NC, NC)

    def yc_peer(e):
        y, c = yc_at(e)
        return {"fsdp": index_of(y, my_z, c)}

    def yc_index(e):
        y, c = yc_at(e)
        return y * NC + c

    def x_peer(d):
        return {"tp": lax.rem(my_x + d, NX)}

    barrier = pltpu.get_barrier_semaphore()
    peers = [x_peer(d) for d in range(1, NX)] + [z_peer(d) for d in range(1, NZ)] + [yc_peer(e) for e in range(1, NYC)]
    for peer in peers:
        pl.semaphore_signal(barrier, inc=1, device_id=peer, device_id_type=MESH)
    own_copies = [
        pltpu.make_async_copy(grads.at[pl.ds(my_x * COLUMN, COLUMN), h], own_part.at[h], loc_sem.at[h]) for h in range(2)
    ]
    mom_copies = [pltpu.make_async_copy(moments.at[:, h], mom.at[h], loc_sem.at[2 + h]) for h in range(2)]
    for copy in own_copies + mom_copies:
        copy.start()
    pl.semaphore_wait(barrier, len(peers))

    rs = []
    for h in range(2):
        row = []
        for d in (2, 1, 3):
            there = lax.rem(my_x + d, NX)
            copy = pltpu.make_async_remote_copy(
                src_ref=grads.at[pl.ds(there * COLUMN, COLUMN), h], dst_ref=parts.at[h, d - 1],
                send_sem=rs_send.at[h, d - 1], recv_sem=rs_recv.at[h, d - 1],
                device_id=x_peer(d), device_id_type=MESH,
            )
            copy.start()
            row.append(copy)
        rs.append(row)
    big_in = [
        pltpu.make_async_copy(left_root, lroot, in_sem.at[0]),
        pltpu.make_async_copy(right_root, rroot, in_sem.at[1]),
        pltpu.make_async_copy(left, lstat, in_sem.at[2]),
        pltpu.make_async_copy(right, rstat, in_sem.at[3]),
        pltpu.make_async_copy(weights, wbuf, in_sem.at[4]),
    ]
    for copy in big_in:
        copy.start()

    chunk = 8
    out_copies = []
    z_copies = [[None] * NZ for _ in range(2)]
    for h in range(2):
        own_copies[h].wait()
        mom_copies[h].wait()
        for copy in rs[h]:
            copy.wait_recv()

        @pl.loop(0, COLUMN // chunk)
        def _(i):
            rows = pl.ds(i * chunk, chunk)
            total = (own_part[h, rows] + parts[h, 0, rows]) + (parts[h, 1, rows] + parts[h, 2, rows])
            total = total * mask[h, rows]
            moment = ADAM_BETA * mom[h, rows] + (1.0 - ADAM_BETA) * total * total
            summed[h][rows] = total
            mom_out[h, rows] = moment
            direction = total / (jnp.sqrt(moment) + ADAM_EPS)
            arow[rows, :] = jnp.sum(direction * direction, axis=1)

        out_copy = pltpu.make_async_copy(mom_out.at[h], new_m.at[:, h], out_sem.at[h])
        out_copy.start()
        out_copies.append(out_copy)
        adam = lax.dot_general(
            jnp.ones((8, COLUMN), F32), arow[...], (((1,), (1,)), ((), ())),
            precision=lax.Precision.HIGHEST, preferred_element_type=F32,
        )[0:4]
        for d in Z_ORDER:
            there = lax.rem(my_z + d, NZ)
            target = zr[h][0] if d == 0 else zsb.at[h, d - 1]
            base = there * cap

            @pl.loop(0, cap, step=8)
            def _(k0):
                for u in range(8):
                    target[k0 + u] = summed[h][zpack[base + k0 + u]]

            target[cap] = adam
            if d:
                copy = pltpu.make_async_remote_copy(
                    src_ref=zsb.at[h, d - 1], dst_ref=zr[h][d],
                    send_sem=z_send.at[h, d - 1], recv_sem=z_recv.at[h, d - 1],
                    device_id=z_peer(d), device_id_type=MESH,
                )
                copy.start()
                z_copies[h][d] = copy

    for h in range(2):
        for d in (0,) + Z_ORDER[:-1]:
            if d:
                z_copies[h][d].wait_recv()
            source_z = lax.rem(my_z + (NZ - d), NZ)
            for e in range(NYC):
                base = yc_index(e) * SLOTS
                target = ysb.at[h, e - 1, d] if e else yr.at[h, my_yc, source_z]
                for j in range(SLOTS):
                    target[j] = zr[h][d][ypack[base + j]]
                target[SLOTS] = zr[h][d][cap]
                if e:
                    pltpu.make_async_remote_copy(
                        src_ref=ysb.at[h, e - 1, d], dst_ref=yr.at[h, my_yc, source_z],
                        send_sem=y_send.at[h], recv_sem=y_recv.at[h],
                        device_id=yc_peer(e), device_id_type=MESH,
                    ).start()

    def y_all(h):
        return pltpu.make_async_remote_copy(
            src_ref=ysb.at[h], dst_ref=yr.at[h, pl.ds(0, NYC - 1)],
            send_sem=y_send.at[h], recv_sem=y_recv.at[h],
            device_id=yc_peer(1), device_id_type=MESH,
        )

    adam_total = jnp.zeros((4, COLUMN), F32)
    for h in range(2):
        y_all(h).wait_recv()

        def build(t, total, h=h):
            y, zs = lax.div(t, NZ), lax.rem(t, NZ)
            for j in range(SLOTS):
                tile = jnp.concatenate([yr[h, y * NC, zs, j], yr[h, y * NC + 1, zs, j]], axis=0)
                tile = jnp.where(own_info[j] > 0, tile, 0.0)
                gfull[j, pl.ds(pl.multiple_of(t * 8, 8), 8), h * HALF:(h + 1) * HALF] = tile
            return total + (yr[h, y * NC, zs, SLOTS] + yr[h, y * NC + 1, zs, SLOTS])

        adam_total = lax.fori_loop(0, NY * NZ, build, adam_total)

    big_in[0].wait()
    big_in[1].wait()
    row_ids = lax.broadcasted_iota(jnp.int32, (2 * HALF, 2 * HALF), 0)
    col_ids = lax.broadcasted_iota(jnp.int32, (2 * HALF, 2 * HALF), 1)
    adam_row = adam_total[0:1]

    @pl.loop(0, SLOTS)
    def _(j):
        high, low = split(gfull[j])
        inner = dot(lroot[j], high) + dot(lroot[j], low)
        in_high, in_low = split(inner)
        prec = dot(in_high, rroot[j]) + dot(in_low, rroot[j])
        live = (row_ids < own_info[8 + j] * HALF) & (col_ids < own_info[16 + j] * HALF)
        prec = jnp.where(live, prec, 0.0)
        prec_sq = jnp.sum(prec * prec)
        adam_sq = jnp.sum(own_hot[pl.ds(j, 1), :] * adam_row)
        graft = LEARN_RATE * jnp.sqrt(jnp.full((1, HALF), adam_sq) / (jnp.full((1, HALF), prec_sq) + NORM_EPS))
        left_cols = (prec[:, :HALF] * graft).reshape(NY * NZ, 8, HALF)
        right_cols = (prec[:, HALF:] * graft).reshape(NY * NZ, 8, HALF)
        for core in range(NC):
            rows = slice(core * 4, core * 4 + 4)
            piece = jnp.concatenate([left_cols[:, rows], right_cols[:, rows]], axis=1)
            for y in range(NY):
                ybs[y * NC + core, :, j] = piece[y * NZ:(y + 1) * NZ]

    for d in Z_ORDER:
        dest_z = lax.rem(my_z + d, NZ)
        for e in range(1, NYC):
            pltpu.make_async_remote_copy(
                src_ref=ybs.at[yc_index(e), dest_z], dst_ref=ybr[d].at[pl.ds(my_yc * SLOTS, SLOTS)],
                send_sem=yb_send, recv_sem=yb_recv.at[d],
                device_id=yc_peer(e), device_id_type=MESH,
            ).start()

    zb_copies = []
    for d in Z_ORDER:
        dest_z = lax.rem(my_z + d, NZ)
        ybr[d][pl.ds(my_yc * SLOTS, SLOTS)] = ybs[my_yc, dest_z]
        pltpu.make_async_remote_copy(
            src_ref=ybr[d].at[pl.ds(0, (NYC - 1) * SLOTS)], dst_ref=ybr[d].at[pl.ds(0, (NYC - 1) * SLOTS)],
            send_sem=yb_send, recv_sem=yb_recv.at[d],
            device_id=yc_peer(1), device_id_type=MESH,
        ).wait_recv()
        target = zbr.at[pl.ds(my_z * cap, cap)] if d == 0 else zbs.at[d - 1]

        @pl.loop(0, cap, step=8)
        def _(k0):
            for u in range(8):
                target[k0 + u] = ybr[d][bpack[k0 + u]]

        if d:
            copy = pltpu.make_async_remote_copy(
                src_ref=zbs.at[d - 1], dst_ref=zbr.at[pl.ds(my_z * cap, cap)],
                send_sem=zb_send.at[d - 1], recv_sem=zb_recv.at[d - 1],
                device_id=z_peer(d), device_id_type=MESH,
            )
            copy.start()
            zb_copies.append(copy)

    big_in[2].wait()
    big_in[3].wait()

    @pl.loop(0, SLOTS)
    def _(j):
        high, low = split(gfull[j])
        rows = ((1,), (1,))
        outer = dot(high, high, rows) + (dot(high, low, rows) + dot(low, high, rows))
        lstat[j] = STAT_BETA * lstat[j] + (1.0 - STAT_BETA) * outer
        cols = ((0,), (0,))
        outer = dot(high, high, cols) + (dot(high, low, cols) + dot(low, high, cols))
        rstat[j] = STAT_BETA * rstat[j] + (1.0 - STAT_BETA) * outer

    for i, (source, out) in enumerate(((lstat, new_left), (rstat, new_right))):
        out_copy = pltpu.make_async_copy(source, out, out_sem.at[2 + i])
        out_copy.start()
        out_copies.append(out_copy)

    big_in[4].wait()
    for copy in zb_copies:
        copy.wait_recv()

    @pl.loop(0, COLUMN, step=8)
    def _(b0):
        for u in range(8):
            new_w[b0 + u] = wbuf[b0 + u] - zbr[home[b0 + u]]

    for h in range(2):
        for copy in rs[h]:
            copy.wait_send()
        for d in range(1, NZ):
            z_copies[h][d].wait_send()
        y_all(h).wait_send()
    pltpu.make_async_remote_copy(
        src_ref=ybs.at[pl.ds(0, NYC - 1)], dst_ref=ybs.at[pl.ds(0, NYC - 1)],
        send_sem=yb_send, recv_sem=yb_recv.at[0],
        device_id=yc_peer(1), device_id_type=MESH,
    ).wait_send()
    for copy in zb_copies:
        copy.wait_send()
    for copy in out_copies:
        copy.wait()


def tables(owner, extent, cap):
    me = lax.axis_index("fsdp").astype(jnp.int32)
    my_z = (me // NC) % NZ
    ids = jnp.arange(COLUMN, dtype=jnp.int32)
    plane = (owner // NC) % NZ
    yc = (owner // (NC * NZ)) * NC + owner % NC
    before = ids[None, :] < ids[:, None]
    rank_owner = jnp.sum((before & (owner[None, :] == owner[:, None])).astype(jnp.int32), axis=1)
    rank_plane = jnp.sum((before & (plane[None, :] == plane[:, None])).astype(jnp.int32), axis=1)
    home = plane * cap + rank_plane
    slot = yc * SLOTS + rank_owner

    def invert(keys, size, values):
        hits = keys[None, :] == jnp.arange(size, dtype=jnp.int32)[:, None]
        return jnp.sum(jnp.where(hits, values[None, :], 0), axis=1)

    here = plane == my_z
    zpack = invert(home, NZ * cap, ids)
    ypack = invert(jnp.where(here, slot, -1), NYC * SLOTS, rank_plane)
    bpack = invert(jnp.where(here, rank_plane, -1), cap, slot)
    mine = jnp.where(owner == me, rank_owner, -1)
    own_hot = (mine[None, :] == jnp.arange(8, dtype=jnp.int32)[:, None])
    own_info = jnp.concatenate([
        jnp.sum(own_hot.astype(jnp.int32), axis=1),
        jnp.sum(jnp.where(own_hot, extent[None, :, 0], 0), axis=1),
        jnp.sum(jnp.where(own_hot, extent[None, :, 1], 0), axis=1),
    ])
    row_live = me * 4 < extent[:, 0] * HALF
    col_live = jnp.arange(2, dtype=jnp.int32)[:, None] < extent[None, :, 1]
    live = (row_live[None, :] & col_live).astype(F32)
    mask = jnp.broadcast_to(live[:, :, None, None], (2, COLUMN, 1, HALF))
    return zpack, ypack, bpack, home, own_info, mask, own_hot.astype(F32)


def run_step(cap, grads, weights, moments, left_stat, right_stat, left_root, right_root, owner, extent):
    piece = (4, HALF)
    any_spec = pl.BlockSpec(memory_space=pl.ANY)
    smem = pl.BlockSpec(memory_space=pltpu.SMEM)
    vmem = pl.BlockSpec(memory_space=pltpu.VMEM)
    size = 2 * HALF
    dma = pltpu.SemaphoreType.DMA
    scratch = (
        [pltpu.VMEM((cap + 1,) + piece, F32) for _ in range(2 * NZ)]
        + [pltpu.VMEM((NYC * SLOTS, 8, HALF), F32) for _ in range(NZ)]
        + [pltpu.VMEM((COLUMN,) + piece, F32) for _ in range(2)]
        + [
            pltpu.VMEM((2, COLUMN) + piece, F32),
            pltpu.VMEM((2, NX - 1, COLUMN) + piece, F32),
            pltpu.VMEM((2, COLUMN) + piece, F32),
            pltpu.VMEM((2, COLUMN) + piece, F32),
            pltpu.VMEM((COLUMN, HALF), F32),
            pltpu.VMEM((2, NZ - 1, cap + 1) + piece, F32),
            pltpu.VMEM((2, NYC - 1, NZ, SLOTS + 1) + piece, F32),
            pltpu.VMEM((2, NYC, NZ, SLOTS + 1) + piece, F32),
            pltpu.VMEM((SLOTS, size, size), F32),
            pltpu.VMEM((SLOTS, size, size), BF16),
            pltpu.VMEM((SLOTS, size, size), BF16),
            pltpu.VMEM((SLOTS, size, size), F32),
            pltpu.VMEM((SLOTS, size, size), F32),
            pltpu.VMEM((NYC, NZ, SLOTS, 8, HALF), F32),
            pltpu.VMEM((NZ - 1, cap, 8, HALF), F32),
            pltpu.VMEM((NZ * cap, 8, HALF), F32),
            pltpu.VMEM((COLUMN, 8, HALF), F32),
            dma((2, NX - 1)), dma((2, NX - 1)),
            dma((2, NZ - 1)), dma((2, NZ - 1)),
            dma((2,)), dma((2,)),
            dma, dma((NZ,)),
            dma((NZ - 1,)), dma((NZ - 1,)),
            dma((4,)), dma((5,)), dma((4,)),
        ]
    )
    halves = lambda a: a.reshape(-1, 4, 2, HALF).transpose(0, 2, 1, 3)
    zpack, ypack, bpack, home, own_info, mask, own_hot = tables(owner, extent, cap)
    new_w, new_m, new_left, new_right = pl.pallas_call(
        functools.partial(step_kernel, cap),
        out_shape=(
            jax.ShapeDtypeStruct((COLUMN, 8, HALF), F32),
            jax.ShapeDtypeStruct((COLUMN, 2) + piece, F32),
            jax.ShapeDtypeStruct((SLOTS, size, size), F32),
            jax.ShapeDtypeStruct((SLOTS, size, size), F32),
        ),
        in_specs=[smem] * 5 + [vmem] * 2 + [any_spec] * 7,
        out_specs=(vmem, any_spec, any_spec, any_spec),
        scratch_shapes=scratch,
        compiler_params=pltpu.CompilerParams(
            collective_id=0, has_side_effects=True, vmem_limit_bytes=48 * 1024 * 1024
        ),
        name="step",
    )(
        zpack, ypack, bpack, home, own_info, mask, own_hot,
        halves(grads[0]), halves(moments), halves(weights).reshape(COLUMN, 8, HALF),
        left_stat[0, 0], right_stat[0, 0], left_root[0, 0], right_root[0, 0],
    )
    whole = lambda a: a.reshape(COLUMN, 2, 4, HALF).transpose(0, 2, 1, 3).reshape(COLUMN, 4, size)
    return whole(new_w), whole(new_m), new_left[None, None], new_right[None, None]


def on_device(*args):
    return run_step(NYC * SLOTS, *args)


def solution(mesh):
    in_specs = (
        P("tp", None, "fsdp", None),
        P("tp", "fsdp", None),
        P("tp", "fsdp", None),
        P("tp", "fsdp", None, None, None),
        P("tp", "fsdp", None, None, None),
        P("tp", "fsdp", None, None, None),
        P("tp", "fsdp", None, None, None),
        P("tp"),
        P("tp", None),
    )
    out_specs = (
        P("tp", "fsdp", None),
        P("tp", "fsdp", None),
        P("tp", "fsdp", None, None, None),
        P("tp", "fsdp", None, None, None),
    )
    return jax.shard_map(
        on_device, mesh=mesh, in_specs=in_specs, out_specs=out_specs, check_vma=False
    )
```

```python
import functools

import jax
import jax.numpy as jnp
from jax import lax
from jax.experimental import pallas as pl
from jax.experimental.pallas import tpu as pltpu
from jax.sharding import PartitionSpec as P

ADAM_BETA = 0.95
STAT_BETA = 0.99
LEARN_RATE = 0.05
ADAM_EPS = 1e-08
NORM_EPS = 1e-06

NX, NY, NZ, NC = 4, 4, 8, 2
NYC = NY * NC
COLUMN = 128
SLOTS = 6
HALF = 128
FULL = NYC * SLOTS
CAPS = (32, FULL)
MESH = pl.DeviceIdType.MESH
Z_ORDER = (4, 3, 5, 2, 6, 1, 7, 0)
F32 = jnp.float32
BF16 = jnp.bfloat16


def split(value):
    high = value.astype(BF16)
    low = (value - high.astype(F32)).astype(BF16)
    return high, low


def dot(a, b, dims=((1,), (0,))):
    return lax.dot_general(a, b, (dims, ((), ())), preferred_element_type=F32)


def step_kernel(
    cap,
    table,
    mask, own_hot, grads, moments, weights, left, right, left_root, right_root,
    new_w, new_m, new_left, new_right,
    *scratch,
):
    scratch = list(scratch)
    zr = [[scratch.pop(0) for _ in range(NZ)] for _ in range(2)]
    ybr = [scratch.pop(0) for _ in range(NZ)]
    summed = [scratch.pop(0) for _ in range(2)]
    (own_part, parts, mom, mom_out, arow, zsb, ysb, yr, gfull, lroot, rroot, lstat, rstat,
     ybs, zbs, zbr, wbuf,
     rs_send, rs_recv, z_send, z_recv, y_send, y_recv, yb_send, yb_recv, zb_send, zb_recv,
     loc_sem, in_sem, out_sem) = scratch

    me = lax.axis_index("fsdp")
    my_x = lax.axis_index("tp")
    my_c = lax.rem(me, NC)
    my_z = lax.rem(lax.div(me, NC), NZ)
    my_y = lax.div(me, NC * NZ)
    my_yc = my_y * NC + my_c

    def index_of(y, z, c):
        return (y * NZ + z) * NC + c

    def z_peer(d):
        return {"fsdp": index_of(my_y, lax.rem(my_z + d, NZ), my_c)}

    def yc_at(e):
        return lax.rem(my_y + e // NC, NY), lax.rem(my_c + e % NC, NC)

    def yc_peer(e):
        y, c = yc_at(e)
        return {"fsdp": index_of(y, my_z, c)}

    def yc_index(e):
        y, c = yc_at(e)
        return y * NC + c

    def x_peer(d):
        return {"tp": lax.rem(my_x + d, NX)}

    barrier = pltpu.get_barrier_semaphore()
    peers = [x_peer(d) for d in range(1, NX)] + [z_peer(d) for d in range(1, NZ)] + [yc_peer(e) for e in range(1, NYC)]
    for peer in peers:
        pl.semaphore_signal(barrier, inc=1, device_id=peer, device_id_type=MESH)
    own_copies = [
        pltpu.make_async_copy(grads.at[pl.ds(my_x * COLUMN, COLUMN), h], own_part.at[h], loc_sem.at[h]) for h in range(2)
    ]
    mom_copies = [pltpu.make_async_copy(moments.at[:, h], mom.at[h], loc_sem.at[2 + h]) for h in range(2)]
    for copy in own_copies + mom_copies:
        copy.start()
    pl.semaphore_wait(barrier, len(peers))

    rs = []
    for h in range(2):
        row = []
        for d in (2, 1, 3):
            there = lax.rem(my_x + d, NX)
            copy = pltpu.make_async_remote_copy(
                src_ref=grads.at[pl.ds(there * COLUMN, COLUMN), h], dst_ref=parts.at[h, d - 1],
                send_sem=rs_send.at[h, d - 1], recv_sem=rs_recv.at[h, d - 1],
                device_id=x_peer(d), device_id_type=MESH,
            )
            copy.start()
            row.append(copy)
        rs.append(row)
    big_in = [
        pltpu.make_async_copy(left_root, lroot, in_sem.at[0]),
        pltpu.make_async_copy(right_root, rroot, in_sem.at[1]),
        pltpu.make_async_copy(left, lstat, in_sem.at[2]),
        pltpu.make_async_copy(right, rstat, in_sem.at[3]),
        pltpu.make_async_copy(weights, wbuf, in_sem.at[4]),
    ]
    for copy in big_in:
        copy.start()

    chunk = 8
    out_copies = []
    z_copies = [[None] * NZ for _ in range(2)]
    for h in range(2):
        own_copies[h].wait()
        mom_copies[h].wait()
        for copy in rs[h]:
            copy.wait_recv()

        @pl.loop(0, COLUMN // chunk)
        def _(i):
            rows = pl.ds(i * chunk, chunk)
            total = (own_part[h, rows] + parts[h, 0, rows]) + (parts[h, 1, rows] + parts[h, 2, rows])
            total = total * mask[h, rows, :].reshape(chunk, 1, HALF)
            moment = ADAM_BETA * mom[h, rows] + (1.0 - ADAM_BETA) * total * total
            summed[h][rows] = total
            mom_out[h, rows] = moment
            direction = total / (jnp.sqrt(moment) + ADAM_EPS)
            arow[rows, :] = jnp.sum(direction * direction, axis=1)

        out_copy = pltpu.make_async_copy(mom_out.at[h], new_m.at[:, h], out_sem.at[h])
        out_copy.start()
        out_copies.append(out_copy)
        adam = lax.dot_general(
            jnp.ones((8, COLUMN), F32), arow[...], (((1,), (1,)), ((), ())),
            precision=lax.Precision.HIGHEST, preferred_element_type=F32,
        )[0:4]
        for d in Z_ORDER:
            there = lax.rem(my_z + d, NZ)
            target = zr[h][0] if d == 0 else zsb.at[h, d - 1]
            base = there * FULL

            @pl.loop(0, cap, step=8)
            def _(k0):
                for u in range(8):
                    target[k0 + u] = summed[h][table[0, base + k0 + u]]

            target[cap] = adam
            if d:
                copy = pltpu.make_async_remote_copy(
                    src_ref=zsb.at[h, d - 1], dst_ref=zr[h][d],
                    send_sem=z_send.at[h, d - 1], recv_sem=z_recv.at[h, d - 1],
                    device_id=z_peer(d), device_id_type=MESH,
                )
                copy.start()
                z_copies[h][d] = copy

    for h in range(2):
        for d in (0,) + Z_ORDER[:-1]:
            if d:
                z_copies[h][d].wait_recv()
            source_z = lax.rem(my_z + (NZ - d), NZ)
            for e in range(NYC):
                base = yc_index(e) * SLOTS
                target = ysb.at[h, e - 1, d] if e else yr.at[h, my_yc, source_z]
                for j in range(SLOTS):
                    target[j] = zr[h][d][table[1, base + j]]
                target[SLOTS] = zr[h][d][cap]
                if e:
                    pltpu.make_async_remote_copy(
                        src_ref=ysb.at[h, e - 1, d], dst_ref=yr.at[h, my_yc, source_z],
                        send_sem=y_send.at[h], recv_sem=y_recv.at[h],
                        device_id=yc_peer(e), device_id_type=MESH,
                    ).start()

    def y_all(h):
        return pltpu.make_async_remote_copy(
            src_ref=ysb.at[h], dst_ref=yr.at[h, pl.ds(0, NYC - 1)],
            send_sem=y_send.at[h], recv_sem=y_recv.at[h],
            device_id=yc_peer(1), device_id_type=MESH,
        )

    adam_total = jnp.zeros((4, COLUMN), F32)
    for h in range(2):
        y_all(h).wait_recv()

        def build(t, total, h=h):
            y, zs = lax.div(t, NZ), lax.rem(t, NZ)
            for j in range(SLOTS):
                tile = jnp.concatenate([yr[h, y * NC, zs, j], yr[h, y * NC + 1, zs, j]], axis=0)
                tile = jnp.where(table[5, j] > 0, tile, 0.0)
                gfull[j, pl.ds(pl.multiple_of(t * 8, 8), 8), h * HALF:(h + 1) * HALF] = tile
            return total + (yr[h, y * NC, zs, SLOTS] + yr[h, y * NC + 1, zs, SLOTS])

        adam_total = lax.fori_loop(0, NY * NZ, build, adam_total)

    big_in[0].wait()
    big_in[1].wait()
    row_ids = lax.broadcasted_iota(jnp.int32, (2 * HALF, 2 * HALF), 0)
    col_ids = lax.broadcasted_iota(jnp.int32, (2 * HALF, 2 * HALF), 1)
    adam_row = adam_total[0:1]

    @pl.loop(0, SLOTS)
    def _(j):
        high, low = split(gfull[j])
        inner = dot(lroot[j], high) + dot(lroot[j], low)
        in_high, in_low = split(inner)
        prec = dot(in_high, rroot[j]) + dot(in_low, rroot[j])
        live = (row_ids < table[6, j] * HALF) & (col_ids < table[7, j] * HALF)
        prec = jnp.where(live, prec, 0.0)
        prec_sq = jnp.sum(prec * prec)
        adam_sq = jnp.sum(own_hot[pl.ds(j, 1), :] * adam_row)
        graft = LEARN_RATE * jnp.sqrt(jnp.full((1, HALF), adam_sq) / (jnp.full((1, HALF), prec_sq) + NORM_EPS))
        left_cols = (prec[:, :HALF] * graft).reshape(NY * NZ, 8, HALF)
        right_cols = (prec[:, HALF:] * graft).reshape(NY * NZ, 8, HALF)
        for core in range(NC):
            rows = slice(core * 4, core * 4 + 4)
            piece = jnp.concatenate([left_cols[:, rows], right_cols[:, rows]], axis=1)
            for y in range(NY):
                ybs[y * NC + core, :, j] = piece[y * NZ:(y + 1) * NZ]

    for d in Z_ORDER:
        dest_z = lax.rem(my_z + d, NZ)
        for e in range(1, NYC):
            pltpu.make_async_remote_copy(
                src_ref=ybs.at[yc_index(e), dest_z], dst_ref=ybr[d].at[pl.ds(my_yc * SLOTS, SLOTS)],
                send_sem=yb_send, recv_sem=yb_recv.at[d],
                device_id=yc_peer(e), device_id_type=MESH,
            ).start()

    zb_copies = []
    for d in Z_ORDER:
        dest_z = lax.rem(my_z + d, NZ)
        ybr[d][pl.ds(my_yc * SLOTS, SLOTS)] = ybs[my_yc, dest_z]
        pltpu.make_async_remote_copy(
            src_ref=ybr[d].at[pl.ds(0, (NYC - 1) * SLOTS)], dst_ref=ybr[d].at[pl.ds(0, (NYC - 1) * SLOTS)],
            send_sem=yb_send, recv_sem=yb_recv.at[d],
            device_id=yc_peer(1), device_id_type=MESH,
        ).wait_recv()
        target = zbr.at[pl.ds(my_z * cap, cap)] if d == 0 else zbs.at[d - 1]

        @pl.loop(0, cap, step=8)
        def _(k0):
            for u in range(8):
                target[k0 + u] = ybr[d][table[2, k0 + u]]

        if d:
            copy = pltpu.make_async_remote_copy(
                src_ref=zbs.at[d - 1], dst_ref=zbr.at[pl.ds(my_z * cap, cap)],
                send_sem=zb_send.at[d - 1], recv_sem=zb_recv.at[d - 1],
                device_id=z_peer(d), device_id_type=MESH,
            )
            copy.start()
            zb_copies.append(copy)

    big_in[2].wait()
    big_in[3].wait()

    @pl.loop(0, SLOTS)
    def _(j):
        high, low = split(gfull[j])
        rows = ((1,), (1,))
        outer = dot(high, high, rows) + (dot(high, low, rows) + dot(low, high, rows))
        lstat[j] = STAT_BETA * lstat[j] + (1.0 - STAT_BETA) * outer
        cols = ((0,), (0,))
        outer = dot(high, high, cols) + (dot(high, low, cols) + dot(low, high, cols))
        rstat[j] = STAT_BETA * rstat[j] + (1.0 - STAT_BETA) * outer

    for i, (source, out) in enumerate(((lstat, new_left), (rstat, new_right))):
        out_copy = pltpu.make_async_copy(source, out, out_sem.at[2 + i])
        out_copy.start()
        out_copies.append(out_copy)

    big_in[4].wait()
    for copy in zb_copies:
        copy.wait_recv()

    @pl.loop(0, COLUMN, step=8)
    def _(b0):
        for u in range(8):
            new_w[b0 + u] = wbuf[b0 + u] - zbr[table[3, b0 + u] * cap + table[4, b0 + u]]

    for h in range(2):
        for copy in rs[h]:
            copy.wait_send()
        for d in range(1, NZ):
            z_copies[h][d].wait_send()
        y_all(h).wait_send()
    pltpu.make_async_remote_copy(
        src_ref=ybs.at[pl.ds(0, NYC - 1)], dst_ref=ybs.at[pl.ds(0, NYC - 1)],
        send_sem=yb_send, recv_sem=yb_recv.at[0],
        device_id=yc_peer(1), device_id_type=MESH,
    ).wait_send()
    for copy in zb_copies:
        copy.wait_send()
    for copy in out_copies:
        copy.wait()


def plan_kernel(owner, extent, table, mask, own_hot, need, mine, theirs, send_sem, recv_sem):
    me = lax.axis_index("fsdp")
    my_x = lax.axis_index("tp")
    my_z = lax.rem(lax.div(me, NC), NZ)
    barrier = pltpu.get_barrier_semaphore()
    peers = [{"tp": lax.rem(my_x + d, NX)} for d in range(1, NX)]
    for peer in peers:
        pl.semaphore_signal(barrier, inc=1, device_id=peer, device_id_type=MESH)

    def down(row):
        return jnp.broadcast_to(row.astype(F32), (COLUMN, COLUMN)).T.astype(jnp.int32)

    own = owner[...]
    plane = lax.rem(lax.div(own, NC), NZ)
    own_t, plane_t = down(own), down(plane)
    earlier = lax.broadcasted_iota(jnp.int32, (COLUMN, COLUMN), 0) < lax.broadcasted_iota(jnp.int32, (COLUMN, COLUMN), 1)

    def rank(keys, keys_t):
        same = earlier & (keys_t == keys)
        return jnp.sum(jnp.where(same, 1.0, 0.0), axis=0, keepdims=True).astype(jnp.int32)

    rank_plane = rank(plane, plane_t)
    mine[...] = jnp.broadcast_to(jnp.max(rank_plane.astype(F32), axis=1, keepdims=True) + 1.0, (8, COLUMN))
    pl.semaphore_wait(barrier, len(peers))
    copies = []
    for d, peer in enumerate(peers):
        copy = pltpu.make_async_remote_copy(
            src_ref=mine, dst_ref=theirs.at[d], send_sem=send_sem.at[d], recv_sem=recv_sem.at[d],
            device_id=peer, device_id_type=MESH,
        )
        copy.start()
        copies.append(copy)

    rank_owner = rank(own, own_t)
    slot = (lax.div(own, NC * NZ) * NC + lax.rem(own, NC)) * SLOTS + rank_owner
    ids_t = lax.broadcasted_iota(jnp.int32, (COLUMN, COLUMN), 0)
    lanes = lax.broadcasted_iota(jnp.int32, (COLUMN, COLUMN), 1)
    zero = jnp.zeros((1, COLUMN), jnp.int32)

    def invert(keys_t, start, values_t):
        hits = keys_t == lanes + start
        return jnp.sum(jnp.where(hits, values_t.astype(F32), 0.0), axis=0, keepdims=True).astype(jnp.int32)

    home_t = down(plane * FULL + rank_plane)
    for i in range(NZ * FULL // COLUMN):
        table[0:1, i * COLUMN:(i + 1) * COLUMN] = invert(home_t, i * COLUMN, ids_t)
    here = plane == my_z
    slot_t, rank_t = down(slot), down(rank_plane)
    mine_t = down(jnp.where(own == me, rank_owner, -1))
    table[1:2, 0:COLUMN] = invert(down(jnp.where(here, slot, -1)), 0, rank_t)
    table[2:3, 0:COLUMN] = invert(down(jnp.where(here, rank_plane, -1)), 0, slot_t)
    table[3:4, 0:COLUMN] = plane
    table[4:5, 0:COLUMN] = rank_plane
    table[5:6, 0:COLUMN] = invert(mine_t, 0, jnp.ones_like(ids_t))
    rows, cols = extent[0:1, :], extent[1:2, :]
    table[6:7, 0:COLUMN] = invert(mine_t, 0, down(rows))
    table[7:8, 0:COLUMN] = invert(mine_t, 0, down(cols))
    row_live = me * 4 < rows * HALF
    for h in range(2):
        mask[h] = down(jnp.where(row_live & (h < cols), 1, 0)).astype(F32)
    here_slot = jnp.broadcast_to(jnp.where(own == me, rank_owner, -1), (8, COLUMN))
    own_hot[...] = jnp.where(here_slot == lax.broadcasted_iota(jnp.int32, (8, COLUMN), 0), 1.0, 0.0)
    for copy in copies:
        copy.wait_recv()
    need[...] = jnp.maximum(jnp.maximum(mine[...], theirs[0]), jnp.maximum(theirs[1], theirs[2]))
    for copy in copies:
        copy.wait_send()


def make_plan(owner, extent):
    vmem = pl.BlockSpec(memory_space=pltpu.VMEM)
    return pl.pallas_call(
        plan_kernel,
        out_shape=(
            jax.ShapeDtypeStruct((8, NZ * FULL), jnp.int32),
            jax.ShapeDtypeStruct((2, COLUMN, HALF), F32),
            jax.ShapeDtypeStruct((8, COLUMN), F32),
            jax.ShapeDtypeStruct((8, COLUMN), F32),
        ),
        in_specs=[vmem] * 2,
        out_specs=(vmem,) * 4,
        scratch_shapes=[
            pltpu.VMEM((8, COLUMN), F32), pltpu.VMEM((NX - 1, 8, COLUMN), F32),
            pltpu.SemaphoreType.DMA((NX - 1,)), pltpu.SemaphoreType.DMA((NX - 1,)),
        ],
        compiler_params=pltpu.CompilerParams(collective_id=0, has_side_effects=True),
        name="plan",
    )(owner.reshape(1, COLUMN), extent.T)


def run_step(cap, table, mask, own_hot, grads, moments, weights, left_stat, right_stat, left_root, right_root):
    piece = (4, HALF)
    any_spec = pl.BlockSpec(memory_space=pl.ANY)
    smem = pl.BlockSpec(memory_space=pltpu.SMEM)
    vmem = pl.BlockSpec(memory_space=pltpu.VMEM)
    size = 2 * HALF
    dma = pltpu.SemaphoreType.DMA
    scratch = (
        [pltpu.VMEM((cap + 1,) + piece, F32) for _ in range(2 * NZ)]
        + [pltpu.VMEM((NYC * SLOTS, 8, HALF), F32) for _ in range(NZ)]
        + [pltpu.VMEM((COLUMN,) + piece, F32) for _ in range(2)]
        + [
            pltpu.VMEM((2, COLUMN) + piece, F32),
            pltpu.VMEM((2, NX - 1, COLUMN) + piece, F32),
            pltpu.VMEM((2, COLUMN) + piece, F32),
            pltpu.VMEM((2, COLUMN) + piece, F32),
            pltpu.VMEM((COLUMN, HALF), F32),
            pltpu.VMEM((2, NZ - 1, cap + 1) + piece, F32),
            pltpu.VMEM((2, NYC - 1, NZ, SLOTS + 1) + piece, F32),
            pltpu.VMEM((2, NYC, NZ, SLOTS + 1) + piece, F32),
            pltpu.VMEM((SLOTS, size, size), F32),
            pltpu.VMEM((SLOTS, size, size), BF16),
            pltpu.VMEM((SLOTS, size, size), BF16),
            pltpu.VMEM((SLOTS, size, size), F32),
            pltpu.VMEM((SLOTS, size, size), F32),
            pltpu.VMEM((NYC, NZ, SLOTS, 8, HALF), F32),
            pltpu.VMEM((NZ - 1, cap, 8, HALF), F32),
            pltpu.VMEM((NZ * cap, 8, HALF), F32),
            pltpu.VMEM((COLUMN, 8, HALF), F32),
            dma((2, NX - 1)), dma((2, NX - 1)),
            dma((2, NZ - 1)), dma((2, NZ - 1)),
            dma((2,)), dma((2,)),
            dma, dma((NZ,)),
            dma((NZ - 1,)), dma((NZ - 1,)),
            dma((4,)), dma((5,)), dma((4,)),
        ]
    )
    halves = lambda a: a.reshape(-1, 4, 2, HALF).transpose(0, 2, 1, 3)
    whole = lambda a: a.reshape(COLUMN, 2, 4, HALF).transpose(0, 2, 1, 3).reshape(COLUMN, 4, size)
    new_w, new_m, new_left, new_right = pl.pallas_call(
        functools.partial(step_kernel, cap),
        out_shape=(
            jax.ShapeDtypeStruct((COLUMN, 8, HALF), F32),
            jax.ShapeDtypeStruct((COLUMN, 2) + piece, F32),
            jax.ShapeDtypeStruct((SLOTS, size, size), F32),
            jax.ShapeDtypeStruct((SLOTS, size, size), F32),
        ),
        in_specs=[smem] + [vmem] * 2 + [any_spec] * 7,
        out_specs=(vmem, any_spec, any_spec, any_spec),
        scratch_shapes=scratch,
        compiler_params=pltpu.CompilerParams(
            collective_id=1 + CAPS.index(cap), has_side_effects=True, vmem_limit_bytes=62 * 1024 * 1024
        ),
        name="step",
    )(
        table, mask, own_hot,
        halves(grads[0]), halves(moments), halves(weights).reshape(COLUMN, 8, HALF),
        left_stat[0, 0], right_stat[0, 0], left_root[0, 0], right_root[0, 0],
    )
    return whole(new_w), whole(new_m), new_left[None, None], new_right[None, None]


def on_device(grads, weights, moments, left_stat, right_stat, left_root, right_root, owner, extent):
    table, mask, own_hot, need = make_plan(owner, extent)
    return lax.cond(
        need[0, 0] <= CAPS[0],
        functools.partial(run_step, CAPS[0]),
        functools.partial(run_step, CAPS[1]),
        table, mask, own_hot, grads, moments, weights, left_stat, right_stat, left_root, right_root,
    )


def solution(mesh):
    in_specs = (
        P("tp", None, "fsdp", None),
        P("tp", "fsdp", None),
        P("tp", "fsdp", None),
        P("tp", "fsdp", None, None, None),
        P("tp", "fsdp", None, None, None),
        P("tp", "fsdp", None, None, None),
        P("tp", "fsdp", None, None, None),
        P("tp"),
        P("tp", None),
    )
    out_specs = (
        P("tp", "fsdp", None),
        P("tp", "fsdp", None),
        P("tp", "fsdp", None, None, None),
        P("tp", "fsdp", None, None, None),
    )
    return jax.shard_map(
        on_device, mesh=mesh, in_specs=in_specs, out_specs=out_specs, check_vma=False
    )
```

```python
import functools

import jax
import jax.numpy as jnp
from jax import lax
from jax.experimental import pallas as pl
from jax.experimental.pallas import tpu as pltpu
from jax.sharding import PartitionSpec as P

ADAM_BETA = 0.95
STAT_BETA = 0.99
LEARN_RATE = 0.05
ADAM_EPS = 1e-08
NORM_EPS = 1e-06

NX, NY, NZ, NC = 4, 4, 8, 2
NYC = NY * NC
COLUMN = 128
SLOTS = 6
HALF = 128
FULL = NYC * SLOTS
EARLY = 2
FIRST = NYC * EARLY
CAPS = (28, 32, FULL)
MESH = pl.DeviceIdType.MESH
Z_ORDER = (4, 3, 5, 2, 6, 1, 7, 0)
F32 = jnp.float32
BF16 = jnp.bfloat16


def split(value):
    high = value.astype(BF16)
    low = (value - high.astype(F32)).astype(BF16)
    return high, low


def dot(a, b, dims=((1,), (0,))):
    return lax.dot_general(a, b, (dims, ((), ())), preferred_element_type=F32)


def units(cap):
    return (
        (0, 0, SLOTS, 1, 0, cap),
        (1, 0, EARLY, 1, 0, FIRST),
        (1, EARLY, SLOTS, 0, FIRST, cap),
    )


PARTS = ((0, EARLY), (EARLY, SLOTS))


def step_kernel(
    cap,
    table, mask, own_hot, grads, moments, weights, left, right, left_root, right_root,
    new_w, new_m, new_left, new_right,
    *scratch,
):
    scratch = list(scratch)
    unit = units(cap)
    zr = [[scratch.pop(0) for _ in range(NZ)] for _ in unit]
    zsb = [scratch.pop(0) for _ in unit]
    ysb = [scratch.pop(0) for _ in unit]
    yr = [scratch.pop(0) for _ in unit]
    ybr = [[scratch.pop(0) for _ in range(NZ)] for _ in PARTS]
    ybs = [scratch.pop(0) for _ in PARTS]
    zbs = [scratch.pop(0) for _ in PARTS]
    summed = [scratch.pop(0) for _ in range(2)]
    (own_part, parts, mom, mom_out, arow, gfull, lroot, rroot, lstat, rstat, zbr, wbuf,
     rs_send, rs_recv, z_send, z_recv, y_send, y_recv, yb_send, yb_recv, zb_send, zb_recv,
     loc_sem, in_sem, out_sem) = scratch

    me = lax.axis_index("fsdp")
    my_x = lax.axis_index("tp")
    my_c = lax.rem(me, NC)
    my_z = lax.rem(lax.div(me, NC), NZ)
    my_y = lax.div(me, NC * NZ)
    my_yc = my_y * NC + my_c

    def index_of(y, z, c):
        return (y * NZ + z) * NC + c

    def z_peer(d):
        return {"fsdp": index_of(my_y, lax.rem(my_z + d, NZ), my_c)}

    def yc_at(e):
        return lax.rem(my_y + e // NC, NY), lax.rem(my_c + e % NC, NC)

    def yc_peer(e):
        y, c = yc_at(e)
        return {"fsdp": index_of(y, my_z, c)}

    def yc_index(e):
        y, c = yc_at(e)
        return y * NC + c

    def x_peer(d):
        return {"tp": lax.rem(my_x + d, NX)}

    def remote(source, target, send, recv, peer):
        return pltpu.make_async_remote_copy(
            src_ref=source, dst_ref=target, send_sem=send, recv_sem=recv, device_id=peer, device_id_type=MESH
        )

    barrier = pltpu.get_barrier_semaphore()
    peers = [x_peer(d) for d in range(1, NX)] + [z_peer(d) for d in range(1, NZ)] + [yc_peer(e) for e in range(1, NYC)]
    for peer in peers:
        pl.semaphore_signal(barrier, inc=1, device_id=peer, device_id_type=MESH)
    own_copies = [
        pltpu.make_async_copy(grads.at[pl.ds(my_x * COLUMN, COLUMN), h], own_part.at[h], loc_sem.at[h]) for h in range(2)
    ]
    mom_copies = [pltpu.make_async_copy(moments.at[:, h], mom.at[h], loc_sem.at[2 + h]) for h in range(2)]
    for copy in own_copies + mom_copies:
        copy.start()
    pl.semaphore_wait(barrier, len(peers))

    rs = []
    for h in range(2):
        row = []
        for d in (2, 1, 3):
            there = lax.rem(my_x + d, NX)
            copy = remote(
                grads.at[pl.ds(there * COLUMN, COLUMN), h], parts.at[h, d - 1],
                rs_send.at[h, d - 1], rs_recv.at[h, d - 1], x_peer(d),
            )
            copy.start()
            row.append(copy)
        rs.append(row)
    big_in = [
        pltpu.make_async_copy(left_root, lroot, in_sem.at[0]),
        pltpu.make_async_copy(right_root, rroot, in_sem.at[1]),
        pltpu.make_async_copy(left, lstat, in_sem.at[2]),
        pltpu.make_async_copy(right, rstat, in_sem.at[3]),
        pltpu.make_async_copy(weights, wbuf, in_sem.at[4]),
    ]
    for copy in big_in:
        copy.start()

    chunk = 8
    out_copies = []

    def sum_half(h):
        own_copies[h].wait()
        mom_copies[h].wait()
        for copy in rs[h]:
            copy.wait_recv()

        @pl.loop(0, COLUMN // chunk)
        def _(i):
            rows = pl.ds(i * chunk, chunk)
            total = (own_part[h, rows] + parts[h, 0, rows]) + (parts[h, 1, rows] + parts[h, 2, rows])
            total = total * mask[h, rows, :].reshape(chunk, 1, HALF)
            moment = ADAM_BETA * mom[h, rows] + (1.0 - ADAM_BETA) * total * total
            summed[h][rows] = total
            mom_out[h, rows] = moment
            direction = total / (jnp.sqrt(moment) + ADAM_EPS)
            arow[rows, :] = jnp.sum(direction * direction, axis=1)

        out_copy = pltpu.make_async_copy(mom_out.at[h], new_m.at[:, h], out_sem.at[h])
        out_copy.start()
        out_copies.append(out_copy)
        return lax.dot_general(
            jnp.ones((8, COLUMN), F32), arow[...], (((1,), (1,)), ((), ())),
            precision=lax.Precision.HIGHEST, preferred_element_type=F32,
        )[0:4]

    def z_out(u, adam):
        h, _, _, with_adam, low, high = unit[u]
        copies = [None] * NZ
        for d in Z_ORDER:
            target = zsb[u].at[d - 1] if d else zr[u][0]
            base = lax.rem(my_z + d, NZ) * FULL + low

            @pl.loop(0, high - low, step=4)
            def _(k0):
                for i in range(4):
                    target[k0 + i] = summed[h][table[0, base + k0 + i]]

            if with_adam:
                target[high - low] = adam
            if d:
                copies[d] = remote(zsb[u].at[d - 1], zr[u][d], z_send.at[u, d - 1], z_recv.at[u, d - 1], z_peer(d))
                copies[d].start()
        return copies

    def y_out(u):
        _, first, last, with_adam, low, high = unit[u]
        for d in (0,) + Z_ORDER[:-1]:
            if d:
                z_copies[u][d].wait_recv()
            source_z = lax.rem(my_z + (NZ - d), NZ)
            for e in range(NYC):
                base = yc_index(e) * SLOTS
                there = yr[u].at[my_yc, source_z]
                target = ysb[u].at[e - 1, d] if e else there
                for j in range(first, last):
                    index = table[1, base + j]
                    target[j - first] = zr[u][d][jnp.maximum(index - low, 0) if low else index]
                if with_adam:
                    target[last - first] = zr[u][d][high - low]
                if e:
                    remote(ysb[u].at[e - 1, d], there, y_send.at[u], y_recv.at[u], yc_peer(e)).start()

    def y_all(u):
        return remote(ysb[u], yr[u].at[pl.ds(0, NYC - 1)], y_send.at[u], y_recv.at[u], yc_peer(1))

    def build(u, total):
        h, first, last, with_adam, _, _ = unit[u]
        y_all(u).wait_recv()

        def body(t, total):
            y, zs = lax.div(t, NZ), lax.rem(t, NZ)
            for j in range(first, last):
                tile = jnp.concatenate([yr[u][y * NC, zs, j - first], yr[u][y * NC + 1, zs, j - first]], axis=0)
                tile = jnp.where(table[5, j] > 0, tile, 0.0)
                gfull[j, pl.ds(pl.multiple_of(t * 8, 8), 8), h * HALF:(h + 1) * HALF] = tile
            if with_adam:
                total = total + (yr[u][y * NC, zs, last - first] + yr[u][y * NC + 1, zs, last - first])
            return total

        return lax.fori_loop(0, NY * NZ, body, total)

    row_ids = lax.broadcasted_iota(jnp.int32, (2 * HALF, 2 * HALF), 0)
    col_ids = lax.broadcasted_iota(jnp.int32, (2 * HALF, 2 * HALF), 1)

    def precondition(p, adam_row):
        first, last = PARTS[p]

        @pl.loop(first, last)
        def _(j):
            high, low = split(gfull[j])
            inner = dot(lroot[j], high) + dot(lroot[j], low)
            in_high, in_low = split(inner)
            prec = dot(in_high, rroot[j]) + dot(in_low, rroot[j])
            live = (row_ids < table[6, j] * HALF) & (col_ids < table[7, j] * HALF)
            prec = jnp.where(live, prec, 0.0)
            prec_sq = jnp.sum(prec * prec)
            adam_sq = jnp.sum(own_hot[pl.ds(j, 1), :] * adam_row)
            graft = LEARN_RATE * jnp.sqrt(jnp.full((1, HALF), adam_sq) / (jnp.full((1, HALF), prec_sq) + NORM_EPS))
            left_cols = (prec[:, :HALF] * graft).reshape(NY * NZ, 8, HALF)
            right_cols = (prec[:, HALF:] * graft).reshape(NY * NZ, 8, HALF)
            for core in range(NC):
                rows = slice(core * 4, core * 4 + 4)
                piece = jnp.concatenate([left_cols[:, rows], right_cols[:, rows]], axis=1)
                for y in range(NY):
                    ybs[p][y * NC + core, :, j - first] = piece[y * NZ:(y + 1) * NZ]

        count = last - first
        for d in Z_ORDER:
            dest_z = lax.rem(my_z + d, NZ)
            for e in range(1, NYC):
                remote(
                    ybs[p].at[yc_index(e), dest_z], ybr[p][d].at[pl.ds(my_yc * count, count)],
                    yb_send.at[p], yb_recv.at[p, d], yc_peer(e),
                ).start()

    zb_copies = []

    def z_back(p):
        first, last = PARTS[p]
        count = last - first
        low, high = (0, FIRST) if p == 0 else (FIRST, cap)
        here = zbr.at[pl.ds(my_z * cap + low, high - low)]
        for d in Z_ORDER:
            dest_z = lax.rem(my_z + d, NZ)
            ybr[p][d][pl.ds(my_yc * count, count)] = ybs[p][my_yc, dest_z]
            arrived = ybr[p][d].at[pl.ds(0, (NYC - 1) * count)]
            remote(arrived, arrived, yb_send.at[p], yb_recv.at[p, d], yc_peer(1)).wait_recv()
            target = zbs[p].at[d - 1] if d else here

            @pl.loop(0, high - low, step=4)
            def _(k0):
                for i in range(4):
                    target[k0 + i] = ybr[p][d][table[2, low + k0 + i]]

            if d:
                copy = remote(zbs[p].at[d - 1], here, zb_send.at[p, d - 1], zb_recv.at[p, d - 1], z_peer(d))
                copy.start()
                zb_copies.append(copy)

    adam = sum_half(0)
    z_copies = [z_out(0, adam)]
    adam = sum_half(1)
    z_copies += [z_out(1, adam), z_out(2, adam)]
    y_out(0)
    y_out(1)
    adam_total = build(0, jnp.zeros((4, COLUMN), F32))
    adam_row = build(1, adam_total)[0:1]
    big_in[0].wait()
    big_in[1].wait()
    precondition(0, adam_row)
    y_out(2)
    z_back(0)
    build(2, adam_total)
    precondition(1, adam_row)
    z_back(1)

    big_in[2].wait()
    big_in[3].wait()

    @pl.loop(0, SLOTS)
    def _(j):
        high, low = split(gfull[j])
        rows = ((1,), (1,))
        outer = dot(high, high, rows) + (dot(high, low, rows) + dot(low, high, rows))
        lstat[j] = STAT_BETA * lstat[j] + (1.0 - STAT_BETA) * outer
        cols = ((0,), (0,))
        outer = dot(high, high, cols) + (dot(high, low, cols) + dot(low, high, cols))
        rstat[j] = STAT_BETA * rstat[j] + (1.0 - STAT_BETA) * outer

    for i, (source, out) in enumerate(((lstat, new_left), (rstat, new_right))):
        out_copy = pltpu.make_async_copy(source, out, out_sem.at[2 + i])
        out_copy.start()
        out_copies.append(out_copy)

    big_in[4].wait()
    for copy in zb_copies:
        copy.wait_recv()

    @pl.loop(0, COLUMN, step=8)
    def _(b0):
        for i in range(8):
            new_w[b0 + i] = wbuf[b0 + i] - zbr[table[3, b0 + i] * cap + table[4, b0 + i]]

    for h in range(2):
        for copy in rs[h]:
            copy.wait_send()
    for u in range(len(unit)):
        for d in range(1, NZ):
            z_copies[u][d].wait_send()
        y_all(u).wait_send()
    for p in range(len(PARTS)):
        sent = ybs[p].at[pl.ds(0, NYC - 1)]
        remote(sent, sent, yb_send.at[p], yb_recv.at[p, 0], yc_peer(1)).wait_send()
    for copy in zb_copies:
        copy.wait_send()
    for copy in out_copies:
        copy.wait()


def plan_kernel(owner, extent, choice, table, mask, own_hot, mine, theirs, send_sem, recv_sem):
    me = lax.axis_index("fsdp")
    my_z = lax.rem(lax.div(me, NC), NZ)
    my_x = lax.axis_index("tp")
    barrier = pltpu.get_barrier_semaphore()
    peers = [{"tp": lax.rem(my_x + d, NX)} for d in range(1, NX)]
    for peer in peers:
        pl.semaphore_signal(barrier, inc=1, device_id=peer, device_id_type=MESH)
    owners = NYC * NZ
    owner_ids = lax.broadcasted_iota(jnp.int32, (owners, COLUMN), 0)
    owned = jnp.where(jnp.broadcast_to(owner[...], (owners, COLUMN)) == owner_ids, 1.0, 0.0)
    excess = jnp.maximum(jnp.sum(owned, axis=1, keepdims=True) - EARLY, 0.0)
    in_plane = lax.rem(lax.div(owner_ids, NC), NZ) == lax.broadcasted_iota(jnp.int32, (owners, COLUMN), 1)
    late_blocks = jnp.sum(jnp.where(in_plane, excess, 0.0), axis=0, keepdims=True)
    mine[...] = jnp.broadcast_to(late_blocks + FIRST, (8, COLUMN))
    pl.semaphore_wait(barrier, len(peers))
    copies = []
    for d, peer in enumerate(peers):
        copy = pltpu.make_async_remote_copy(
            src_ref=mine, dst_ref=theirs.at[d], send_sem=send_sem.at[d], recv_sem=recv_sem.at[d],
            device_id=peer, device_id_type=MESH,
        )
        copy.start()
        copies.append(copy)
    fill_tables(me, my_z, owner, extent, table, mask, own_hot)
    for copy in copies:
        copy.wait_recv()
    need = jnp.max(jnp.maximum(jnp.maximum(mine[...], theirs[0]), jnp.maximum(theirs[1], theirs[2])))
    index = jnp.int32(0)
    for cap in CAPS[:-1]:
        index = index + jnp.where(need > cap, jnp.int32(1), jnp.int32(0))
    choice[0, 0] = index
    for copy in copies:
        copy.wait_send()


def make_plan(owner, extent):
    vmem = pl.BlockSpec(memory_space=pltpu.VMEM)
    return pl.pallas_call(
        plan_kernel,
        out_shape=(
            jax.ShapeDtypeStruct((1, 1), jnp.int32),
            jax.ShapeDtypeStruct((8, NZ * FULL), jnp.int32),
            jax.ShapeDtypeStruct((2, COLUMN, HALF), F32),
            jax.ShapeDtypeStruct((8, COLUMN), F32),
        ),
        in_specs=[vmem] * 2,
        out_specs=(pl.BlockSpec(memory_space=pltpu.SMEM), vmem, vmem, vmem),
        scratch_shapes=[
            pltpu.VMEM((8, COLUMN), F32), pltpu.VMEM((NX - 1, 8, COLUMN), F32),
            pltpu.SemaphoreType.DMA((NX - 1,)), pltpu.SemaphoreType.DMA((NX - 1,)),
        ],
        compiler_params=pltpu.CompilerParams(collective_id=0, has_side_effects=True),
        name="plan",
    )(owner, extent)


def fill_tables(me, my_z, owner, extent, table, mask, own_hot):
    def down(row):
        return jnp.broadcast_to(row.astype(F32), (COLUMN, COLUMN)).T.astype(jnp.int32)

    own = owner[...]
    plane = lax.rem(lax.div(own, NC), NZ)
    own_t = down(own)
    ids_t = lax.broadcasted_iota(jnp.int32, (COLUMN, COLUMN), 0)
    lanes = lax.broadcasted_iota(jnp.int32, (COLUMN, COLUMN), 1)
    earlier = ids_t < lanes

    def rank(keys, keys_t):
        same = earlier & (keys_t == keys)
        return jnp.sum(jnp.where(same, 1.0, 0.0), axis=0, keepdims=True).astype(jnp.int32)

    def invert(keys_t, start, values_t):
        hits = keys_t == lanes + start
        return jnp.sum(jnp.where(hits, values_t.astype(F32), 0.0), axis=0, keepdims=True).astype(jnp.int32)

    rank_owner = rank(own, own_t)
    late = jnp.where(rank_owner >= EARLY, 1, 0)
    key = plane * 2 + late
    rank_plane = rank(key, down(key)) + late * FIRST
    yc = lax.div(own, NC * NZ) * NC + lax.rem(own, NC)
    slot = yc * SLOTS + rank_owner
    slot_in_part = jnp.where(late > 0, yc * (SLOTS - EARLY) + rank_owner - EARLY, yc * EARLY + rank_owner)
    home_t = down(plane * FULL + rank_plane)
    for i in range(NZ * FULL // COLUMN):
        table[0:1, i * COLUMN:(i + 1) * COLUMN] = invert(home_t, i * COLUMN, ids_t)
    here = plane == my_z
    rank_t = down(rank_plane)
    mine = jnp.where(own == me, rank_owner, -1)
    mine_t = down(mine)
    table[1:2, 0:COLUMN] = invert(down(jnp.where(here, slot, -1)), 0, rank_t)
    table[2:3, 0:COLUMN] = invert(down(jnp.where(here, rank_plane, -1)), 0, down(slot_in_part))
    table[3:4, 0:COLUMN] = plane
    table[4:5, 0:COLUMN] = rank_plane
    table[5:6, 0:COLUMN] = invert(mine_t, 0, jnp.ones_like(ids_t))
    rows, cols = extent[0:1, :], extent[1:2, :]
    table[6:7, 0:COLUMN] = invert(mine_t, 0, down(rows))
    table[7:8, 0:COLUMN] = invert(mine_t, 0, down(cols))
    row_live = me * 4 < rows * HALF
    for h in range(2):
        mask[h] = down(jnp.where(row_live & (h < cols), 1, 0)).astype(F32)
    here_slot = jnp.broadcast_to(mine, (8, COLUMN))
    own_hot[...] = jnp.where(here_slot == lax.broadcasted_iota(jnp.int32, (8, COLUMN), 0), 1.0, 0.0)


def run_step(cap, table, mask, own_hot, grads, moments, weights, left_stat, right_stat, left_root, right_root):
    piece = (4, HALF)
    any_spec = pl.BlockSpec(memory_space=pl.ANY)
    hbm = pl.BlockSpec(memory_space=pltpu.HBM)
    vmem = pl.BlockSpec(memory_space=pltpu.VMEM)
    size = 2 * HALF
    dma = pltpu.SemaphoreType.DMA
    unit = units(cap)
    pieces = [high - low + with_adam for _, _, _, with_adam, low, high in unit]
    slots = [last - first + with_adam for _, first, last, with_adam, _, _ in unit]
    part_slots = [last - first for first, last in PARTS]
    home_pieces = [FIRST, cap - FIRST]
    scratch = (
        [pltpu.VMEM((n,) + piece, F32) for n in pieces for _ in range(NZ)]
        + [pltpu.VMEM((NZ - 1, n) + piece, F32) for n in pieces]
        + [pltpu.VMEM((NYC - 1, NZ, n) + piece, F32) for n in slots]
        + [pltpu.VMEM((NYC, NZ, n) + piece, F32) for n in slots]
        + [pltpu.VMEM((NYC * n, 8, HALF), F32) for n in part_slots for _ in range(NZ)]
        + [pltpu.VMEM((NYC, NZ, n, 8, HALF), F32) for n in part_slots]
        + [pltpu.VMEM((NZ - 1, n, 8, HALF), F32) for n in home_pieces]
        + [pltpu.VMEM((COLUMN,) + piece, F32) for _ in range(2)]
        + [
            pltpu.VMEM((2, COLUMN) + piece, F32),
            pltpu.VMEM((2, NX - 1, COLUMN) + piece, F32),
            pltpu.VMEM((2, COLUMN) + piece, F32),
            pltpu.VMEM((2, COLUMN) + piece, F32),
            pltpu.VMEM((COLUMN, HALF), F32),
            pltpu.VMEM((SLOTS, size, size), F32),
            pltpu.VMEM((SLOTS, size, size), BF16),
            pltpu.VMEM((SLOTS, size, size), BF16),
            pltpu.VMEM((SLOTS, size, size), F32),
            pltpu.VMEM((SLOTS, size, size), F32),
            pltpu.VMEM((NZ * cap, 8, HALF), F32),
            pltpu.VMEM((COLUMN, 8, HALF), F32),
            dma((2, NX - 1)), dma((2, NX - 1)),
            dma((3, NZ - 1)), dma((3, NZ - 1)),
            dma((3,)), dma((3,)),
            dma((2,)), dma((2, NZ)),
            dma((2, NZ - 1)), dma((2, NZ - 1)),
            dma((4,)), dma((5,)), dma((4,)),
        ]
    )
    halves = lambda a: a.reshape(-1, 4, 2, HALF).transpose(0, 2, 1, 3)
    whole = lambda a: a.reshape(COLUMN, 2, 4, HALF).transpose(0, 2, 1, 3).reshape(COLUMN, 4, size)
    new_w, new_m, new_left, new_right = pl.pallas_call(
        functools.partial(step_kernel, cap),
        out_shape=(
            jax.ShapeDtypeStruct((COLUMN, 8, HALF), F32),
            jax.ShapeDtypeStruct((COLUMN, 2) + piece, F32),
            jax.ShapeDtypeStruct((SLOTS, size, size), F32),
            jax.ShapeDtypeStruct((SLOTS, size, size), F32),
        ),
        in_specs=[pl.BlockSpec(memory_space=pltpu.SMEM)] + [vmem] * 2 + [hbm] * 7,
        out_specs=(vmem, any_spec, any_spec, any_spec),
        scratch_shapes=scratch,
        compiler_params=pltpu.CompilerParams(
            collective_id=1 + CAPS.index(cap), has_side_effects=True, vmem_limit_bytes=30 * 1024 * 1024
        ),
        name="step",
    )(
        table, mask, own_hot,
        halves(grads[0]), halves(moments), halves(weights).reshape(COLUMN, 8, HALF),
        left_stat[0, 0], right_stat[0, 0], left_root[0, 0], right_root[0, 0],
    )
    return whole(new_w), whole(new_m), new_left[None, None], new_right[None, None]


def on_device(grads, weights, moments, left_stat, right_stat, left_root, right_root, owner, extent):
    choice, table, mask, own_hot = make_plan(owner.reshape(1, COLUMN), extent.T)
    return lax.switch(
        choice[0, 0],
        [functools.partial(run_step, cap) for cap in CAPS],
        table, mask, own_hot, grads, moments, weights, left_stat, right_stat, left_root, right_root,
    )


def solution(mesh):
    in_specs = (
        P("tp", None, "fsdp", None),
        P("tp", "fsdp", None),
        P("tp", "fsdp", None),
        P("tp", "fsdp", None, None, None),
        P("tp", "fsdp", None, None, None),
        P("tp", "fsdp", None, None, None),
        P("tp", "fsdp", None, None, None),
        P("tp"),
        P("tp", None),
    )
    out_specs = (
        P("tp", "fsdp", None),
        P("tp", "fsdp", None),
        P("tp", "fsdp", None, None, None),
        P("tp", "fsdp", None, None, None),
    )
    return jax.shard_map(
        on_device, mesh=mesh, in_specs=in_specs, out_specs=out_specs, check_vma=False
    )
```

```python
import functools

import jax
import jax.numpy as jnp
from jax import lax
from jax.experimental import pallas as pl
from jax.experimental.pallas import tpu as pltpu
from jax.sharding import PartitionSpec as P

ADAM_BETA = 0.95
STAT_BETA = 0.99
LEARN_RATE = 0.05
ADAM_EPS = 1e-08
NORM_EPS = 1e-06

NX, NY, NZ, NC = 4, 4, 8, 2
NYC = NY * NC
COLUMN = 128
SLOTS = 6
HALF = 128
FULL = NYC * SLOTS
EARLY = 2
FIRST = NYC * EARLY
CAPS = (28, 32, FULL)
MESH = pl.DeviceIdType.MESH
Z_ORDER = (4, 3, 5, 2, 6, 1, 7, 0)
F32 = jnp.float32
BF16 = jnp.bfloat16


def split(value):
    high = value.astype(BF16)
    low = (value - high.astype(F32)).astype(BF16)
    return high, low


def dot(a, b, dims=((1,), (0,))):
    return lax.dot_general(a, b, (dims, ((), ())), preferred_element_type=F32)


def units(cap):
    return (
        (0, 0, SLOTS, 1, 0, cap),
        (1, 0, EARLY, 1, 0, FIRST),
        (1, EARLY, SLOTS, 0, FIRST, cap),
    )


PARTS = ((0, EARLY), (EARLY, SLOTS))


def step_kernel(
    cap,
    table, mask, own_hot, grads, moments, weights, left, right, left_root, right_root,
    new_w, new_m, new_left, new_right,
    *scratch,
):
    scratch = list(scratch)
    unit = units(cap)
    zr = [[scratch.pop(0) for _ in range(NZ)] for _ in unit]
    zsb = [scratch.pop(0) for _ in unit]
    ysb = [scratch.pop(0) for _ in unit]
    yr = [scratch.pop(0) for _ in unit]
    ybr = [[scratch.pop(0) for _ in range(NZ)] for _ in PARTS]
    ybs = [scratch.pop(0) for _ in PARTS]
    zbs = [scratch.pop(0) for _ in PARTS]
    summed = [scratch.pop(0) for _ in range(2)]
    (own_part, parts, mom, mom_out, arow, gfull, lroot, rroot, lstat, rstat, zbr, wbuf,
     rs_send, rs_recv, z_send, z_recv, y_send, y_recv, yb_send, yb_recv, zb_send, zb_recv,
     loc_sem, in_sem, out_sem) = scratch

    me = lax.axis_index("fsdp")
    my_x = lax.axis_index("tp")
    my_c = lax.rem(me, NC)
    my_z = lax.rem(lax.div(me, NC), NZ)
    my_y = lax.div(me, NC * NZ)
    my_yc = my_y * NC + my_c

    def index_of(y, z, c):
        return (y * NZ + z) * NC + c

    def z_peer(d):
        return {"fsdp": index_of(my_y, lax.rem(my_z + d, NZ), my_c)}

    def yc_at(e):
        return lax.rem(my_y + e // NC, NY), lax.rem(my_c + e % NC, NC)

    def yc_peer(e):
        y, c = yc_at(e)
        return {"fsdp": index_of(y, my_z, c)}

    def yc_index(e):
        y, c = yc_at(e)
        return y * NC + c

    def x_peer(d):
        return {"tp": lax.rem(my_x + d, NX)}

    def remote(source, target, send, recv, peer):
        return pltpu.make_async_remote_copy(
            src_ref=source, dst_ref=target, send_sem=send, recv_sem=recv, device_id=peer, device_id_type=MESH
        )

    barrier = pltpu.get_barrier_semaphore()
    peers = [x_peer(d) for d in range(1, NX)] + [z_peer(d) for d in range(1, NZ)] + [yc_peer(e) for e in range(1, NYC)]
    for peer in peers:
        pl.semaphore_signal(barrier, inc=1, device_id=peer, device_id_type=MESH)
    own_copies = [
        pltpu.make_async_copy(grads.at[pl.ds(my_x * COLUMN, COLUMN), h], own_part.at[h], loc_sem.at[h]) for h in range(2)
    ]
    mom_copies = [pltpu.make_async_copy(moments.at[:, h], mom.at[h], loc_sem.at[2 + h]) for h in range(2)]
    for copy in own_copies + mom_copies:
        copy.start()
    pl.semaphore_wait(barrier, len(peers))

    rs = []
    for h in range(2):
        row = []
        for d in (2, 1, 3):
            there = lax.rem(my_x + d, NX)
            copy = remote(
                grads.at[pl.ds(there * COLUMN, COLUMN), h], parts.at[h, d - 1],
                rs_send.at[h, d - 1], rs_recv.at[h, d - 1], x_peer(d),
            )
            copy.start()
            row.append(copy)
        rs.append(row)
    big_in = [
        pltpu.make_async_copy(left_root, lroot, in_sem.at[0]),
        pltpu.make_async_copy(right_root, rroot, in_sem.at[1]),
        pltpu.make_async_copy(left, lstat, in_sem.at[2]),
        pltpu.make_async_copy(right, rstat, in_sem.at[3]),
        pltpu.make_async_copy(weights, wbuf, in_sem.at[4]),
    ]
    for copy in big_in:
        copy.start()

    chunk = 8
    out_copies = []

    def sum_half(h):
        own_copies[h].wait()
        mom_copies[h].wait()
        for copy in rs[h]:
            copy.wait_recv()

        @pl.loop(0, COLUMN // chunk)
        def _(i):
            rows = pl.ds(i * chunk, chunk)
            total = (own_part[h, rows] + parts[h, 0, rows]) + (parts[h, 1, rows] + parts[h, 2, rows])
            total = total * mask[h, rows, :].reshape(chunk, 1, HALF)
            moment = ADAM_BETA * mom[h, rows] + (1.0 - ADAM_BETA) * total * total
            summed[h][rows] = total
            mom_out[h, rows] = moment
            direction = total / (jnp.sqrt(moment) + ADAM_EPS)
            arow[rows, :] = jnp.sum(direction * direction, axis=1)

        out_copy = pltpu.make_async_copy(mom_out.at[h], new_m.at[:, h], out_sem.at[h])
        out_copy.start()
        out_copies.append(out_copy)
        return lax.dot_general(
            jnp.ones((8, COLUMN), F32), arow[...], (((1,), (1,)), ((), ())),
            precision=lax.Precision.HIGHEST, preferred_element_type=F32,
        )[0:4]

    def z_out(u, adam):
        h, _, _, with_adam, low, high = unit[u]
        copies = [None] * NZ
        for d in Z_ORDER:
            target = zsb[u].at[d - 1] if d else zr[u][0]
            base = lax.rem(my_z + d, NZ) * FULL + low

            @pl.loop(0, high - low, step=4)
            def _(k0):
                for i in range(4):
                    target[k0 + i] = summed[h][table[0, base + k0 + i]]

            if with_adam:
                target[high - low] = adam
            if d:
                copies[d] = remote(zsb[u].at[d - 1], zr[u][d], z_send.at[u, d - 1], z_recv.at[u, d - 1], z_peer(d))
                copies[d].start()
        return copies

    def y_out(u):
        _, first, last, with_adam, low, high = unit[u]
        for d in (0,) + Z_ORDER[:-1]:
            if d:
                z_copies[u][d].wait_recv()
            source_z = lax.rem(my_z + (NZ - d), NZ)
            for e in range(NYC):
                base = yc_index(e) * SLOTS
                there = yr[u].at[my_yc, source_z]
                target = ysb[u].at[e - 1, d] if e else there
                for j in range(first, last):
                    index = table[1, base + j]
                    target[j - first] = zr[u][d][jnp.maximum(index - low, 0) if low else index]
                if with_adam:
                    target[last - first] = zr[u][d][high - low]
                if e:
                    remote(ysb[u].at[e - 1, d], there, y_send.at[u], y_recv.at[u], yc_peer(e)).start()

    def y_all(u):
        return remote(ysb[u], yr[u].at[pl.ds(0, NYC - 1)], y_send.at[u], y_recv.at[u], yc_peer(1))

    def build(u, total):
        h, first, last, with_adam, _, _ = unit[u]
        y_all(u).wait_recv()

        def body(t, total):
            y, zs = lax.div(t, NZ), lax.rem(t, NZ)
            for j in range(first, last):
                tile = jnp.concatenate([yr[u][y * NC, zs, j - first], yr[u][y * NC + 1, zs, j - first]], axis=0)
                tile = jnp.where(table[5, j] > 0, tile, 0.0)
                gfull[j, pl.ds(pl.multiple_of(t * 8, 8), 8), h * HALF:(h + 1) * HALF] = tile
            if with_adam:
                total = total + (yr[u][y * NC, zs, last - first] + yr[u][y * NC + 1, zs, last - first])
            return total

        return lax.fori_loop(0, NY * NZ, body, total)

    row_ids = lax.broadcasted_iota(jnp.int32, (2 * HALF, 2 * HALF), 0)
    col_ids = lax.broadcasted_iota(jnp.int32, (2 * HALF, 2 * HALF), 1)

    def precondition(p, adam_row):
        first, last = PARTS[p]

        @pl.loop(first, last, unroll=True)
        def _(j):
            high, low = split(gfull[j])
            inner = dot(lroot[j], high) + dot(lroot[j], low)
            in_high, in_low = split(inner)
            prec = dot(in_high, rroot[j]) + dot(in_low, rroot[j])
            live = (row_ids < table[6, j] * HALF) & (col_ids < table[7, j] * HALF)
            prec = jnp.where(live, prec, 0.0)
            prec_sq = jnp.sum(prec * prec)
            adam_sq = jnp.sum(own_hot[pl.ds(j, 1), :] * adam_row)
            graft = LEARN_RATE * jnp.sqrt(jnp.full((1, HALF), adam_sq) / (jnp.full((1, HALF), prec_sq) + NORM_EPS))
            left_cols = (prec[:, :HALF] * graft).reshape(NY * NZ, 8, HALF)
            right_cols = (prec[:, HALF:] * graft).reshape(NY * NZ, 8, HALF)
            for core in range(NC):
                rows = slice(core * 4, core * 4 + 4)
                piece = jnp.concatenate([left_cols[:, rows], right_cols[:, rows]], axis=1)
                for y in range(NY):
                    ybs[p][y * NC + core, :, j - first] = piece[y * NZ:(y + 1) * NZ]

        count = last - first
        for d in Z_ORDER:
            dest_z = lax.rem(my_z + d, NZ)
            for e in range(1, NYC):
                remote(
                    ybs[p].at[yc_index(e), dest_z], ybr[p][d].at[pl.ds(my_yc * count, count)],
                    yb_send.at[p], yb_recv.at[p, d], yc_peer(e),
                ).start()

    zb_copies = []

    def z_back(p):
        first, last = PARTS[p]
        count = last - first
        low, high = (0, FIRST) if p == 0 else (FIRST, cap)
        here = zbr.at[pl.ds(my_z * cap + low, high - low)]
        for d in Z_ORDER:
            dest_z = lax.rem(my_z + d, NZ)
            ybr[p][d][pl.ds(my_yc * count, count)] = ybs[p][my_yc, dest_z]
            arrived = ybr[p][d].at[pl.ds(0, (NYC - 1) * count)]
            remote(arrived, arrived, yb_send.at[p], yb_recv.at[p, d], yc_peer(1)).wait_recv()
            target = zbs[p].at[d - 1] if d else here

            @pl.loop(0, high - low, step=4)
            def _(k0):
                for i in range(4):
                    target[k0 + i] = ybr[p][d][table[2, low + k0 + i]]

            if d:
                copy = remote(zbs[p].at[d - 1], here, zb_send.at[p, d - 1], zb_recv.at[p, d - 1], z_peer(d))
                copy.start()
                zb_copies.append(copy)

    adam = sum_half(0)
    z_copies = [z_out(0, adam)]
    adam = sum_half(1)
    z_copies += [z_out(1, adam), z_out(2, adam)]
    y_out(0)
    y_out(1)
    adam_total = build(0, jnp.zeros((4, COLUMN), F32))
    adam_row = build(1, adam_total)[0:1]
    big_in[0].wait()
    big_in[1].wait()
    precondition(0, adam_row)
    y_out(2)
    z_back(0)
    build(2, adam_total)
    precondition(1, adam_row)
    z_back(1)

    big_in[2].wait()
    big_in[3].wait()

    @pl.loop(0, SLOTS)
    def _(j):
        high, low = split(gfull[j])
        rows = ((1,), (1,))
        outer = dot(high, high, rows) + (dot(high, low, rows) + dot(low, high, rows))
        lstat[j] = STAT_BETA * lstat[j] + (1.0 - STAT_BETA) * outer
        cols = ((0,), (0,))
        outer = dot(high, high, cols) + (dot(high, low, cols) + dot(low, high, cols))
        rstat[j] = STAT_BETA * rstat[j] + (1.0 - STAT_BETA) * outer

    for i, (source, out) in enumerate(((lstat, new_left), (rstat, new_right))):
        out_copy = pltpu.make_async_copy(source, out, out_sem.at[2 + i])
        out_copy.start()
        out_copies.append(out_copy)

    big_in[4].wait()
    for copy in zb_copies:
        copy.wait_recv()

    @pl.loop(0, COLUMN, step=8)
    def _(b0):
        for i in range(8):
            new_w[b0 + i] = wbuf[b0 + i] - zbr[table[3, b0 + i] * cap + table[4, b0 + i]]

    for h in range(2):
        for copy in rs[h]:
            copy.wait_send()
    for u in range(len(unit)):
        for d in range(1, NZ):
            z_copies[u][d].wait_send()
        y_all(u).wait_send()
    for p in range(len(PARTS)):
        sent = ybs[p].at[pl.ds(0, NYC - 1)]
        remote(sent, sent, yb_send.at[p], yb_recv.at[p, 0], yc_peer(1)).wait_send()
    for copy in zb_copies:
        copy.wait_send()
    for copy in out_copies:
        copy.wait()


def plan_kernel(owner, extent, choice, table, mask, own_hot, mine, theirs, send_sem, recv_sem):
    me = lax.axis_index("fsdp")
    my_z = lax.rem(lax.div(me, NC), NZ)
    my_x = lax.axis_index("tp")
    barrier = pltpu.get_barrier_semaphore()
    peers = [{"tp": lax.rem(my_x + d, NX)} for d in range(1, NX)]
    for peer in peers:
        pl.semaphore_signal(barrier, inc=1, device_id=peer, device_id_type=MESH)
    owners = NYC * NZ
    owner_ids = lax.broadcasted_iota(jnp.int32, (owners, COLUMN), 0)
    owned = jnp.where(jnp.broadcast_to(owner[...], (owners, COLUMN)) == owner_ids, 1.0, 0.0)
    excess = jnp.maximum(jnp.sum(owned, axis=1, keepdims=True) - EARLY, 0.0)
    in_plane = lax.rem(lax.div(owner_ids, NC), NZ) == lax.broadcasted_iota(jnp.int32, (owners, COLUMN), 1)
    late_blocks = jnp.sum(jnp.where(in_plane, excess, 0.0), axis=0, keepdims=True)
    mine[...] = jnp.broadcast_to(late_blocks + FIRST, (8, COLUMN))
    pl.semaphore_wait(barrier, len(peers))
    copies = []
    for d, peer in enumerate(peers):
        copy = pltpu.make_async_remote_copy(
            src_ref=mine, dst_ref=theirs.at[d], send_sem=send_sem.at[d], recv_sem=recv_sem.at[d],
            device_id=peer, device_id_type=MESH,
        )
        copy.start()
        copies.append(copy)
    fill_tables(me, my_z, owner, extent, table, mask, own_hot)
    for copy in copies:
        copy.wait_recv()
    need = jnp.max(jnp.maximum(jnp.maximum(mine[...], theirs[0]), jnp.maximum(theirs[1], theirs[2])))
    index = jnp.int32(0)
    for cap in CAPS[:-1]:
        index = index + jnp.where(need > cap, jnp.int32(1), jnp.int32(0))
    choice[0, 0] = index
    for copy in copies:
        copy.wait_send()


def make_plan(owner, extent):
    vmem = pl.BlockSpec(memory_space=pltpu.VMEM)
    return pl.pallas_call(
        plan_kernel,
        out_shape=(
            jax.ShapeDtypeStruct((1, 1), jnp.int32),
            jax.ShapeDtypeStruct((8, NZ * FULL), jnp.int32),
            jax.ShapeDtypeStruct((2, COLUMN, HALF), F32),
            jax.ShapeDtypeStruct((8, COLUMN), F32),
        ),
        in_specs=[vmem] * 2,
        out_specs=(pl.BlockSpec(memory_space=pltpu.SMEM), vmem, vmem, vmem),
        scratch_shapes=[
            pltpu.VMEM((8, COLUMN), F32), pltpu.VMEM((NX - 1, 8, COLUMN), F32),
            pltpu.SemaphoreType.DMA((NX - 1,)), pltpu.SemaphoreType.DMA((NX - 1,)),
        ],
        compiler_params=pltpu.CompilerParams(collective_id=0, has_side_effects=True),
        name="plan",
    )(owner, extent)


def fill_tables(me, my_z, owner, extent, table, mask, own_hot):
    def down(row):
        return jnp.broadcast_to(row.astype(F32), (COLUMN, COLUMN)).T.astype(jnp.int32)

    own = owner[...]
    plane = lax.rem(lax.div(own, NC), NZ)
    own_t = down(own)
    ids_t = lax.broadcasted_iota(jnp.int32, (COLUMN, COLUMN), 0)
    lanes = lax.broadcasted_iota(jnp.int32, (COLUMN, COLUMN), 1)
    earlier = ids_t < lanes

    def rank(keys, keys_t):
        same = earlier & (keys_t == keys)
        return jnp.sum(jnp.where(same, 1.0, 0.0), axis=0, keepdims=True).astype(jnp.int32)

    def invert(keys_t, start, values_t):
        hits = keys_t == lanes + start
        return jnp.sum(jnp.where(hits, values_t.astype(F32), 0.0), axis=0, keepdims=True).astype(jnp.int32)

    rank_owner = rank(own, own_t)
    late = jnp.where(rank_owner >= EARLY, 1, 0)
    key = plane * 2 + late
    rank_plane = rank(key, down(key)) + late * FIRST
    yc = lax.div(own, NC * NZ) * NC + lax.rem(own, NC)
    slot = yc * SLOTS + rank_owner
    slot_in_part = jnp.where(late > 0, yc * (SLOTS - EARLY) + rank_owner - EARLY, yc * EARLY + rank_owner)
    home_t = down(plane * FULL + rank_plane)
    for i in range(NZ * FULL // COLUMN):
        table[0:1, i * COLUMN:(i + 1) * COLUMN] = invert(home_t, i * COLUMN, ids_t)
    here = plane == my_z
    rank_t = down(rank_plane)
    mine = jnp.where(own == me, rank_owner, -1)
    mine_t = down(mine)
    table[1:2, 0:COLUMN] = invert(down(jnp.where(here, slot, -1)), 0, rank_t)
    table[2:3, 0:COLUMN] = invert(down(jnp.where(here, rank_plane, -1)), 0, down(slot_in_part))
    table[3:4, 0:COLUMN] = plane
    table[4:5, 0:COLUMN] = rank_plane
    table[5:6, 0:COLUMN] = invert(mine_t, 0, jnp.ones_like(ids_t))
    rows, cols = extent[0:1, :], extent[1:2, :]
    table[6:7, 0:COLUMN] = invert(mine_t, 0, down(rows))
    table[7:8, 0:COLUMN] = invert(mine_t, 0, down(cols))
    row_live = me * 4 < rows * HALF
    for h in range(2):
        mask[h] = down(jnp.where(row_live & (h < cols), 1, 0)).astype(F32)
    here_slot = jnp.broadcast_to(mine, (8, COLUMN))
    own_hot[...] = jnp.where(here_slot == lax.broadcasted_iota(jnp.int32, (8, COLUMN), 0), 1.0, 0.0)


def run_step(cap, table, mask, own_hot, grads, moments, weights, left_stat, right_stat, left_root, right_root):
    piece = (4, HALF)
    any_spec = pl.BlockSpec(memory_space=pl.ANY)
    hbm = pl.BlockSpec(memory_space=pltpu.HBM)
    vmem = pl.BlockSpec(memory_space=pltpu.VMEM)
    size = 2 * HALF
    dma = pltpu.SemaphoreType.DMA
    unit = units(cap)
    pieces = [high - low + with_adam for _, _, _, with_adam, low, high in unit]
    slots = [last - first + with_adam for _, first, last, with_adam, _, _ in unit]
    part_slots = [last - first for first, last in PARTS]
    home_pieces = [FIRST, cap - FIRST]
    scratch = (
        [pltpu.VMEM((n,) + piece, F32) for n in pieces for _ in range(NZ)]
        + [pltpu.VMEM((NZ - 1, n) + piece, F32) for n in pieces]
        + [pltpu.VMEM((NYC - 1, NZ, n) + piece, F32) for n in slots]
        + [pltpu.VMEM((NYC, NZ, n) + piece, F32) for n in slots]
        + [pltpu.VMEM((NYC * n, 8, HALF), F32) for n in part_slots for _ in range(NZ)]
        + [pltpu.VMEM((NYC, NZ, n, 8, HALF), F32) for n in part_slots]
        + [pltpu.VMEM((NZ - 1, n, 8, HALF), F32) for n in home_pieces]
        + [pltpu.VMEM((COLUMN,) + piece, F32) for _ in range(2)]
        + [
            pltpu.VMEM((2, COLUMN) + piece, F32),
            pltpu.VMEM((2, NX - 1, COLUMN) + piece, F32),
            pltpu.VMEM((2, COLUMN) + piece, F32),
            pltpu.VMEM((2, COLUMN) + piece, F32),
            pltpu.VMEM((COLUMN, HALF), F32),
            pltpu.VMEM((SLOTS, size, size), F32),
            pltpu.VMEM((SLOTS, size, size), BF16),
            pltpu.VMEM((SLOTS, size, size), BF16),
            pltpu.VMEM((SLOTS, size, size), F32),
            pltpu.VMEM((SLOTS, size, size), F32),
            pltpu.VMEM((NZ * cap, 8, HALF), F32),
            pltpu.VMEM((COLUMN, 8, HALF), F32),
            dma((2, NX - 1)), dma((2, NX - 1)),
            dma((3, NZ - 1)), dma((3, NZ - 1)),
            dma((3,)), dma((3,)),
            dma((2,)), dma((2, NZ)),
            dma((2, NZ - 1)), dma((2, NZ - 1)),
            dma((4,)), dma((5,)), dma((4,)),
        ]
    )
    halves = lambda a: a.reshape(-1, 4, 2, HALF).transpose(0, 2, 1, 3)
    whole = lambda a: a.reshape(COLUMN, 2, 4, HALF).transpose(0, 2, 1, 3).reshape(COLUMN, 4, size)
    new_w, new_m, new_left, new_right = pl.pallas_call(
        functools.partial(step_kernel, cap),
        out_shape=(
            jax.ShapeDtypeStruct((COLUMN, 8, HALF), F32),
            jax.ShapeDtypeStruct((COLUMN, 2) + piece, F32),
            jax.ShapeDtypeStruct((SLOTS, size, size), F32),
            jax.ShapeDtypeStruct((SLOTS, size, size), F32),
        ),
        in_specs=[pl.BlockSpec(memory_space=pltpu.SMEM)] + [vmem] * 2 + [hbm] * 7,
        out_specs=(vmem, any_spec, any_spec, any_spec),
        scratch_shapes=scratch,
        compiler_params=pltpu.CompilerParams(
            collective_id=1 + CAPS.index(cap), has_side_effects=True, vmem_limit_bytes=30 * 1024 * 1024
        ),
        name="step",
    )(
        table, mask, own_hot,
        halves(grads[0]), halves(moments), halves(weights).reshape(COLUMN, 8, HALF),
        left_stat[0, 0], right_stat[0, 0], left_root[0, 0], right_root[0, 0],
    )
    return whole(new_w), whole(new_m), new_left[None, None], new_right[None, None]


def on_device(grads, weights, moments, left_stat, right_stat, left_root, right_root, owner, extent):
    choice, table, mask, own_hot = make_plan(owner.reshape(1, COLUMN), extent.T)
    return lax.switch(
        choice[0, 0],
        [functools.partial(run_step, cap) for cap in CAPS],
        table, mask, own_hot, grads, moments, weights, left_stat, right_stat, left_root, right_root,
    )


def solution(mesh):
    in_specs = (
        P("tp", None, "fsdp", None),
        P("tp", "fsdp", None),
        P("tp", "fsdp", None),
        P("tp", "fsdp", None, None, None),
        P("tp", "fsdp", None, None, None),
        P("tp", "fsdp", None, None, None),
        P("tp", "fsdp", None, None, None),
        P("tp"),
        P("tp", None),
    )
    out_specs = (
        P("tp", "fsdp", None),
        P("tp", "fsdp", None),
        P("tp", "fsdp", None, None, None),
        P("tp", "fsdp", None, None, None),
    )
    return jax.shard_map(
        on_device, mesh=mesh, in_specs=in_specs, out_specs=out_specs, check_vma=False
    )
```
